32 devices in a mesh: dp: 8 (over y, x, core), tensor: 4 (over z).
Axes of the slice: x: 2, y: 2, z: 4, core: 2. Of those that a mesh axis runs over, the one named last changes fastest.
Arguments:
- hidden_states: float32 [2048, 1024], P('dp'), may hold values from -6 to 6
- output_cotangent: float32 [2048, 1024], P('dp'), may hold values from -6 to 6
- routes: int32 [2048, 8], P('dp'), may hold values from 0 to 31, all different within a row; in each aligned block of 256 rows (0 to 255, 256 to 511, ...) at most 96 rows name the same one
- attention_gain: float32 [2, 1024], replicated, may hold values from 0.5 to 1.5
- query_weight: bfloat16 [2, 1024, 1024], P(None, None, 'tensor'), may hold values from -0.1875 to 0.1875
- key_weight: bfloat16 [2, 512, 1024], P(None, 'tensor'), may hold values from -0.1875 to 0.1875
- value_weight: bfloat16 [2, 512, 1024], P(None, 'tensor'), may hold values from -0.1875 to 0.1875
- output_weight: bfloat16 [2, 1024, 1024], P(None, 'tensor'), may hold values from -4 to 4
- mixture_gain: float32 [2, 1024], replicated, may hold values from 0.5 to 1.5
- router_weight: bfloat16 [2, 1024, 32], replicated, may hold values from -0.046875 to 0.046875
- gate_weight: bfloat16 [2, 32, 512, 1024], P(None, 'dp', 'tensor'), may hold values from -0.1875 to 0.1875
- up_weight: bfloat16 [2, 32, 512, 1024], P(None, 'dp', 'tensor'), may hold values from -0.1875 to 0.1875
- down_weight: bfloat16 [2, 32, 512, 1024], P(None, 'dp', 'tensor'), may hold values from -6 to 6
Outputs:
- block_output: float32 [2048, 1024], P('dp')
- input_gradient: float32 [2048, 1024], P('dp')
- attention_gain_gradient: float32 [2, 1024], P(None, 'dp')
- query_gradient: float32 [2, 1024, 1024], P(None, 'dp', 'tensor')
- key_gradient: float32 [2, 512, 1024], P(None, 'tensor', 'dp')
- value_gradient: float32 [2, 512, 1024], P(None, 'tensor', 'dp')
- projection_gradient: float32 [2, 1024, 1024], P(None, 'tensor', 'dp')
- mixture_gain_gradient: float32 [2, 1024], P(None, 'dp')
- router_gradient: float32 [2, 1024, 32], P(None, 'dp')
- gate_gradient: float32 [2, 32, 512, 1024], P(None, 'dp', 'tensor')
- up_gradient: float32 [2, 32, 512, 1024], P(None, 'dp', 'tensor')
- down_gradient: float32 [2, 32, 512, 1024], P(None, 'dp', 'tensor')
The draws below stay inside these ranges and needn't reach their ends.
Inputs may be any that keep to these rules, and one draw needn't show every extreme that they name: `routes`: each row names 8 different experts; among the rows of one block of 256 rows no expert is named more than 96 times, a bound that some block reaches.
All inputs are finite; a program needn't handle non-finite values.
Results may differ from the reference program's by a relative error of at most 0.02.
Values may be sent and summed in bfloat16 or wider, within the bound.
A program may use at most 256 MiB of HBM per device.

```python
import math
import jax
import jax.numpy as jnp
import numpy as np
from jax import lax

D = 1024
H = 16
KV = 8
HD = 64
EXPERTS = 32
FF = 512
TOPK = 8
LAYERS = 2
SEQ = 256
TOK_DEV = 256
TOKENS = 2048
CAP = 96
N_DP = 8


def with_spikes(entries, own_key, source, target, parts, factor):
    owner, partner = [(jnp.arange(entries.shape[dim]) // (entries.shape[dim] // parts)).reshape([-1 if axis == dim else 1 for axis in range(entries.ndim)]) for dim in (source, target)]
    chosen = jax.random.permutation(own_key, parts)[partner]
    strong = (owner == chosen) | (owner == (partner + parts // 2) % parts)
    return jnp.where(strong, factor * entries, entries)


def steps_of(key, shape, shards, low, top_value):
    factor_of = 1.0
    for dim, blocks in shards:
        draws = jax.random.uniform(jax.random.fold_in(jax.random.fold_in(key, 6), dim), (blocks,), jnp.float32, low / len(shards), top_value / len(shards))
        factor_of = factor_of * jnp.repeat(jnp.exp(draws), shape[dim] // blocks).reshape((-1,) + (1,) * (len(shape) - 1 - dim))
    return factor_of


def routed_block(stream_key, own, number, rows, number_of, top, limit, lean):
    order = jax.random.permutation(stream_key, number_of)
    crowded, common = portions_of(number_of, rows * top, limit, lean, True), portions_of(number_of, rows * top, limit, lean, False)
    places = jnp.arange(number_of)

    def named(sizes, turn):
        used = int((sizes > 0).sum())
        fixed = max(1, used // 4)
        moved = fixed + (places - fixed + turn * (used - fixed)) % max(1, number_of - fixed)
        return jnp.zeros((number_of,), jnp.int32).at[order[jnp.where(places < fixed, places, moved)]].set(jnp.asarray(sizes, jnp.int32))

    sizes = jnp.where(number % 4 == 0, named(crowded, number // 4), named(common, number - number // 4 - 1))
    mixed = jax.random.permutation(jax.random.fold_in(own, 3), number_of)
    giver, taker = mixed[0:number_of // 2 * 2:2], mixed[1:number_of // 2 * 2:2]
    margin = jnp.minimum(sizes[giver] - 1, limit - sizes[taker]) // 2
    margin = jnp.where((giver == order[0]) | (taker == order[0]) | (sizes[taker] == 0), 0, jnp.maximum(margin, 0))
    moved = jax.random.randint(jax.random.fold_in(own, 4), (number_of // 2,), 0, 1 << 20) % (margin + 1)
    sizes = sizes.at[giver].add(-moved).at[taker].add(moved)
    items = jnp.searchsorted(jnp.cumsum(sizes), jnp.arange(rows * top), side="right").astype(jnp.int32)
    listing = items.reshape(top, rows).T
    listing = listing[jax.random.permutation(jax.random.fold_in(own, 1), rows)]
    turn = jax.random.randint(jax.random.fold_in(own, 2), (rows, 1), 0, top)
    return jnp.take_along_axis(listing, (jnp.arange(top)[None, :] + turn) % top, axis=1)


def portions_of(number_of, total, reach, skew, full):
    weights = [(1 << 20) // math.isqrt(rank ** skew) + 1 for rank in range(1, number_of + 1)]
    largest = reach if full else min(reach, max(-(-total // number_of), total * weights[0] // sum(weights)))
    least = 1 if total - largest >= number_of - 1 else 0
    given, spare = [largest] + [least] * (number_of - 1), total - largest - least * (number_of - 1)
    while spare > 0:
        candidates = [i for i in range(1, number_of) if given[i] < largest] or [i for i in range(1, number_of) if given[i] < reach]
        whole, remaining = sum([weights[i] for i in candidates]), spare
        for i in candidates:
            addition = min(reach - given[i], max(1, remaining * weights[i] // whole), spare)
            given[i] = given[i] + addition
            spare = spare - addition
    return np.array(given)


def noise(key, dims, scale, most, cuts=(), kind=jnp.bfloat16):
    factor_of = steps_of(key, dims, cuts, -0.22, 0.18) if cuts else 1.0
    array = jax.random.normal(key, dims, jnp.float32) * scale * factor_of
    return jnp.minimum(jnp.maximum(array, -most), most).astype(kind)


def noise_with(own_key, shape, deviation, reach, cuts, heavy, held_as=jnp.bfloat16):
    values = deviation * jax.random.normal(own_key, shape, jnp.float32)
    if cuts:
        values = values * steps_of(own_key, shape, cuts, -0.22, 0.18)
    return jnp.clip(with_spikes(values, jax.random.fold_in(own_key, 3), *heavy), -reach, reach).astype(held_as)


def setup_inputs(seed: int = 0) -> dict:
    key_list = jax.random.split(jax.random.key(seed), 14)
    hidden_states = noise_with(key_list[0], (TOKENS, D), 1.0, 6.0, ((0, 8),), (0, 1, 8, 2.0), jnp.float32)
    output_cotangent = noise_with(key_list[1], (TOKENS, D), 1.0, 6.0, ((0, 8),), (0, 1, 8, 2.0), jnp.float32)
    routes_keys = jax.random.split(jax.random.fold_in(key_list[2], 1), TOKENS // TOK_DEV)
    routes_turns = jax.random.permutation(jax.random.fold_in(key_list[2], 3), TOKENS // TOK_DEV)
    routes = jax.vmap(lambda own, number: routed_block(jax.random.fold_in(key_list[2], 2), own, number, TOK_DEV, EXPERTS, TOPK, CAP, 2))(routes_keys, routes_turns).reshape((TOKENS, TOPK))
    attention_gain = jnp.clip(1.0 + 0.1 * jax.random.normal(key_list[3], (LAYERS, D), jnp.float32), 0.5, 1.5)
    query_weight = noise(key_list[4], (LAYERS, D, H * HD), D ** -0.5, 0.1875, ((2, 4),))
    key_weight = noise(key_list[5], (LAYERS, KV * HD, D), D ** -0.5, 0.1875, ((1, 4),))
    value_weight = noise(key_list[6], (LAYERS, KV * HD, D), D ** -0.5, 0.1875, ((1, 4),))
    output_weight = noise(key_list[7], (LAYERS, H * HD, D), 2 ** -0.5, 4.0, ((1, 4),))
    mixture_gain = jnp.clip(1.0 + 0.1 * jax.random.normal(key_list[8], (LAYERS, D), jnp.float32), 0.5, 1.5)
    router_weight = noise(key_list[9], (LAYERS, D, EXPERTS), (16 * D) ** -0.5, 0.046875)
    gate_weight = noise(key_list[10], (LAYERS, EXPERTS, FF, D), D ** -0.5, 0.1875, ((1, 8), (2, 4)))
    up_weight = noise(key_list[11], (LAYERS, EXPERTS, FF, D), D ** -0.5, 0.1875, ((1, 8), (2, 4)))
    down_weight = noise(key_list[12], (LAYERS, EXPERTS, FF, D), 1 ** -0.5, 6.0, ((1, 8), (2, 4)))
    return {"hidden_states": hidden_states, "output_cotangent": output_cotangent, "routes": routes, "attention_gain": attention_gain, "query_weight": query_weight, "key_weight": key_weight, "value_weight": value_weight, "output_weight": output_weight, "mixture_gain": mixture_gain, "router_weight": router_weight, "gate_weight": gate_weight, "up_weight": up_weight, "down_weight": down_weight}


EPSILON = 1e-06
RESIDUAL_SCALE = 0.22
SCORE_SCALE = 0.015625
ROPE_BASE = 10000.0
NEG_LARGE = -1e+30

def rotate_half(values):
    middle = values.shape[-1] // 2
    return jnp.concatenate([-values[..., middle:], values[..., :middle]], axis=-1)

def rope_tables(row_count):
    middle = HD // 2
    positions = (jnp.arange(row_count, dtype=jnp.int32) % SEQ).astype(jnp.float32)
    inverse_rate = ROPE_BASE ** (-(jnp.arange(middle, dtype=jnp.int32).astype(jnp.float32) * (2.0 / HD)))
    angles = positions[:, None] * inverse_rate[None, :]
    cosine = jnp.concatenate([jnp.cos(angles), jnp.cos(angles)], axis=1)[:, None, :]
    sine = jnp.concatenate([jnp.sin(angles), jnp.sin(angles)], axis=1)[:, None, :]
    return (cosine, sine)

def causal_mask():
    counter = jnp.arange(SEQ, dtype=jnp.int32)
    return counter[:, None] >= counter[None, :]

def dot_full(left, right):
    return jnp.dot(left, right, precision=lax.Precision.HIGHEST, preferred_element_type=jnp.float32)

def float_einsum(form, left, right):
    return jnp.einsum(form, left.astype(jnp.float32), right.astype(jnp.float32), preferred_element_type=jnp.float32)

def slot_targets(routes, experts):
    flat_routes = routes.reshape(-1)
    onehot = (flat_routes[:, None] == jnp.arange(experts, dtype=jnp.int32)[None, :]).astype(jnp.int32)
    before = jnp.cumsum(onehot, axis=0) - onehot
    slot_index = lax.optimization_barrier(jnp.sum(before * onehot, axis=1))
    return (flat_routes * CAP + slot_index).astype(jnp.int32).reshape(routes.shape)

def norm_forward(source, gain):
    inverse_root = lax.rsqrt(lax.optimization_barrier(jnp.mean(source * source, axis=1, keepdims=True)) + EPSILON)
    return (inverse_root, source * inverse_root * gain)

def norm_backward(grad_in, source, inverse_root, gain):
    gain_grad = lax.optimization_barrier(jnp.sum(grad_in * source * inverse_root, axis=0))
    scaled = grad_in * gain
    inner = lax.optimization_barrier(jnp.mean(scaled * source, axis=1, keepdims=True))
    return (inverse_root * (scaled - source * inverse_root * inverse_root * inner), gain_grad)

def attend_forward(query, keys, values):
    scores = float_einsum('sqkgd,stkd->skgqt', query, keys) * SCORE_SCALE
    scores = jnp.where(causal_mask(), scores, NEG_LARGE)
    highest = lax.optimization_barrier(jnp.max(scores, axis=-1, keepdims=True))
    weights = jnp.exp(scores - highest)
    totals = lax.optimization_barrier(jnp.sum(weights, axis=-1, keepdims=True))
    log_total = highest + jnp.log(totals)
    probability = (weights / totals).astype(jnp.bfloat16)
    attended = float_einsum('skgqt,stkd->sqkgd', probability, values)
    return (attended.astype(jnp.bfloat16), log_total)

def attend_backward(query, keys, values, attended, log_total, grad_out):
    scores = float_einsum('sqkgd,stkd->skgqt', query, keys) * SCORE_SCALE
    scores = jnp.where(causal_mask(), scores, NEG_LARGE)
    probability = jnp.exp(scores - log_total)
    value_grad = float_einsum('skgqt,sqkgd->stkd', probability.astype(jnp.bfloat16), grad_out)
    prob_grad = float_einsum('sqkgd,stkd->skgqt', grad_out, values)
    delta_rows = lax.optimization_barrier(jnp.sum(grad_out.astype(jnp.float32) * attended.astype(jnp.float32), axis=-1))
    delta_rows = jnp.transpose(delta_rows, (0, 2, 3, 1))[..., None]
    score_grad = (probability * (prob_grad - delta_rows)).astype(jnp.bfloat16)
    query_grad = float_einsum('skgqt,stkd->sqkgd', score_grad, keys) * SCORE_SCALE
    key_grad = float_einsum('skgqt,sqkgd->stkd', score_grad, query) * SCORE_SCALE
    return (query_grad, key_grad, value_grad)

def router_backward(weight_grad, router_probs, chosen):
    prob_grad = lax.optimization_barrier(jnp.sum(chosen * weight_grad[:, :, None], axis=1))
    return router_probs * (prob_grad - lax.optimization_barrier(jnp.sum(router_probs * prob_grad, axis=1, keepdims=True)))

def layer_forward(inputs, params, targets, chosen, cosine, sine):
    attention_gain, query_weight, key_weight, value_weight, output_weight, mixture_gain, router_weight, gate_weight, up_weight, down_weight = params
    row_count, width = inputs.shape
    query_heads = query_weight.shape[1] // HD
    key_heads = key_weight.shape[0] // HD
    group_size = query_heads // key_heads
    seq_count = row_count // SEQ
    first_scale, first_normed = norm_forward(inputs, attention_gain)
    first_input = first_normed.astype(jnp.bfloat16)
    query = jnp.dot(first_input, query_weight, preferred_element_type=jnp.float32).reshape(row_count, query_heads, HD)
    keys = jnp.dot(first_input, key_weight.T, preferred_element_type=jnp.float32).reshape(row_count, key_heads, HD)
    values = jnp.dot(first_input, value_weight.T, preferred_element_type=jnp.float32).astype(jnp.bfloat16)
    query = (query * cosine + rotate_half(query) * sine).astype(jnp.bfloat16)
    keys = (keys * cosine + rotate_half(keys) * sine).astype(jnp.bfloat16)
    query_split = query.reshape(seq_count, SEQ, key_heads, group_size, HD)
    key_split = keys.reshape(seq_count, SEQ, key_heads, HD)
    value_split = values.reshape(seq_count, SEQ, key_heads, HD)
    attended, log_total = attend_forward(query_split, key_split, value_split)
    attended_rows = attended.reshape(row_count, query_heads * HD)
    attention_out = jnp.dot(attended_rows, output_weight, preferred_element_type=jnp.float32)
    middle_state = inputs + RESIDUAL_SCALE * attention_out
    second_scale, second_normed = norm_forward(middle_state, mixture_gain)
    second_input = second_normed.astype(jnp.bfloat16)
    logits = jnp.dot(second_input, router_weight, preferred_element_type=jnp.float32)
    router_probs = jax.nn.softmax(logits, axis=1)
    route_weights = lax.optimization_barrier(jnp.sum(chosen * router_probs[:, None, :], axis=2))
    experts = gate_weight.shape[0]
    flat_targets = targets.reshape(-1)
    dispatched = jnp.zeros((experts * CAP, width), jnp.bfloat16).at[flat_targets].set(jnp.repeat(second_input, TOPK, axis=0)).reshape(experts, CAP, width)
    gate_pre = float_einsum('ecd,efd->ecf', dispatched, gate_weight)
    up_pre = float_einsum('ecd,efd->ecf', dispatched, up_weight)
    activated = (jax.nn.silu(gate_pre) * up_pre).astype(jnp.bfloat16)
    expert_out = float_einsum('ecf,efd->ecd', activated, down_weight).reshape(experts * CAP, width)
    picked = expert_out[targets]
    mixture_out = lax.optimization_barrier(jnp.sum(route_weights[:, :, None] * picked, axis=1))
    outputs = middle_state + RESIDUAL_SCALE * mixture_out
    saved = (first_scale, first_input, query_split, key_split, value_split, attended, log_total, middle_state, second_scale, second_input, router_probs, route_weights, dispatched, gate_pre, up_pre, activated, picked)
    return (outputs, saved)

def layer_backward(grad_out, saved, params, targets, chosen, cosine, sine, inputs):
    attention_gain, query_weight, key_weight, value_weight, output_weight, mixture_gain, router_weight, gate_weight, up_weight, down_weight = params
    first_scale, first_input, query_split, key_split, value_split, attended, log_total, middle_state, second_scale, second_input, router_probs, route_weights, dispatched, gate_pre, up_pre, activated, picked = saved
    row_count, width = grad_out.shape
    query_heads = query_weight.shape[1] // HD
    key_heads = key_weight.shape[0] // HD
    experts = gate_weight.shape[0]
    mixture_grad = RESIDUAL_SCALE * grad_out
    weight_grad = lax.optimization_barrier(jnp.sum(mixture_grad[:, None, :] * picked, axis=2))
    spread = (route_weights[:, :, None] * mixture_grad[:, None, :]).astype(jnp.bfloat16).reshape(row_count * TOPK, width)
    out_grad = jnp.zeros((experts * CAP, width), jnp.bfloat16).at[targets.reshape(-1)].set(spread).reshape(experts, CAP, width)
    act_grad = float_einsum('ecd,efd->ecf', out_grad, down_weight)
    down_grad = float_einsum('ecf,ecd->efd', activated, out_grad)
    sigma = jax.nn.sigmoid(gate_pre)
    gate_rows = (act_grad * up_pre * sigma * (1.0 + gate_pre * (1.0 - sigma))).astype(jnp.bfloat16)
    up_rows = (act_grad * gate_pre * sigma).astype(jnp.bfloat16)
    gate_grad = float_einsum('ecf,ecd->efd', gate_rows, dispatched)
    up_grad = float_einsum('ecf,ecd->efd', up_rows, dispatched)
    dispatch_grad = (float_einsum('ecf,efd->ecd', gate_rows, gate_weight) + float_einsum('ecf,efd->ecd', up_rows, up_weight)).reshape(experts * CAP, width)
    input_part = lax.optimization_barrier(jnp.sum(dispatch_grad[targets], axis=1))
    logit_grad = router_backward(weight_grad, router_probs, chosen)
    second_grad = input_part + dot_full(logit_grad, router_weight.astype(jnp.float32).T)
    router_grad = dot_full(second_input.astype(jnp.float32).T, logit_grad)
    middle_norm_grad, mixture_gain_grad = norm_backward(second_grad, middle_state, second_scale, mixture_gain)
    middle_grad = grad_out + middle_norm_grad
    attention_grad = (RESIDUAL_SCALE * middle_grad).astype(jnp.bfloat16)
    attended_rows = attended.reshape(row_count, query_heads * HD)
    output_grad = jnp.dot(attended_rows.T, attention_grad, preferred_element_type=jnp.float32)
    attended_grad = jnp.dot(attention_grad, output_weight.T, preferred_element_type=jnp.float32).astype(jnp.bfloat16)
    query_grad, key_grad, value_grad = attend_backward(query_split, key_split, value_split, attended, log_total, attended_grad.reshape(attended.shape))
    query_grad = query_grad.reshape(row_count, query_heads, HD)
    query_grad = (query_grad * cosine - rotate_half(query_grad) * sine).astype(jnp.bfloat16).reshape(row_count, query_heads * HD)
    key_grad = key_grad.reshape(row_count, key_heads, HD)
    key_grad = (key_grad * cosine - rotate_half(key_grad) * sine).astype(jnp.bfloat16).reshape(row_count, key_heads * HD)
    value_grad = value_grad.astype(jnp.bfloat16).reshape(row_count, key_heads * HD)
    query_weight_grad = jnp.dot(first_input.T, query_grad, preferred_element_type=jnp.float32)
    key_weight_grad = jnp.dot(key_grad.T, first_input, preferred_element_type=jnp.float32)
    value_weight_grad = jnp.dot(value_grad.T, first_input, preferred_element_type=jnp.float32)
    first_grad = jnp.dot(query_grad, query_weight.T, preferred_element_type=jnp.float32) + jnp.dot(key_grad, key_weight, preferred_element_type=jnp.float32) + jnp.dot(value_grad, value_weight, preferred_element_type=jnp.float32)
    input_norm_grad, attention_gain_grad = norm_backward(first_grad, inputs, first_scale, attention_gain)
    input_grad = middle_grad + input_norm_grad
    return (input_grad, (attention_gain_grad, query_weight_grad, key_weight_grad, value_weight_grad, output_grad, mixture_gain_grad, router_grad, gate_grad, up_grad, down_grad))

def reference(hidden_states, output_cotangent, routes, attention_gain, query_weight, key_weight, value_weight, output_weight, mixture_gain, router_weight, gate_weight, up_weight, down_weight):
    params_all = (attention_gain, query_weight, key_weight, value_weight, output_weight, mixture_gain, router_weight, gate_weight, up_weight, down_weight)
    cosine, sine = rope_tables(TOK_DEV)

    def one_block(totals, block):
        states, cotangent, block_routes = block
        targets = slot_targets(block_routes, EXPERTS)
        chosen = (block_routes[:, :, None] == jnp.arange(EXPERTS, dtype=jnp.int32)[None, None, :]).astype(jnp.float32)
        current = states
        kept = []
        for layer_index in range(LAYERS):
            layer_params = tuple((weight[layer_index] for weight in params_all))
            layer_input = current
            current, saved = layer_forward(current, layer_params, targets, chosen, cosine, sine)
            kept.append((saved, layer_input))
        grad_now = cotangent
        per_layer = [None] * LAYERS
        for layer_index in reversed(range(LAYERS)):
            layer_params = tuple((weight[layer_index] for weight in params_all))
            grad_now, grads = layer_backward(grad_now, kept[layer_index][0], layer_params, targets, chosen, cosine, sine, kept[layer_index][1])
            per_layer[layer_index] = grads
        new_totals = tuple((totals[position] + jnp.stack([entry[position] for entry in per_layer]) for position in range(10)))
        return (new_totals, (current, grad_now))
    zero_totals = tuple((jnp.zeros(weight.shape, jnp.float32) for weight in params_all))
    blocks = (hidden_states.reshape(N_DP, TOK_DEV, D), output_cotangent.reshape(N_DP, TOK_DEV, D), routes.reshape(N_DP, TOK_DEV, TOPK))
    totals, (outputs, gradients) = lax.scan(one_block, zero_totals, blocks)
    return (outputs.reshape(TOKENS, D), gradients.reshape(TOKENS, D), totals[0], totals[1], totals[2], totals[3], totals[4], totals[5], totals[6], totals[7], totals[8], totals[9])
```

```python
import functools

import jax
import jax.numpy as jnp
from jax import lax
from jax.experimental import pallas as pl
from jax.experimental.pallas import tpu as pltpu
from jax.sharding import PartitionSpec as P

HD = 64
EXPERTS = 32
SEQ = 256


EPSILON = 1e-06
RESIDUAL_SCALE = 0.22
SCORE_SCALE = 0.015625
ROPE_BASE = 10000.0
NEG_LARGE = -1e30


def rotate_half(values):
    middle = values.shape[-1] // 2
    return jnp.concatenate([-values[..., middle:], values[..., :middle]], axis=-1)


def rope_tables(row_count):
    middle = HD // 2
    positions = (jnp.arange(row_count, dtype=jnp.int32) % SEQ).astype(jnp.float32)
    inverse_rate = ROPE_BASE ** (
        -(jnp.arange(middle, dtype=jnp.int32).astype(jnp.float32) * (2.0 / HD))
    )
    angles = positions[:, None] * inverse_rate[None, :]
    cosine = jnp.concatenate([jnp.cos(angles), jnp.cos(angles)], axis=1)[:, None, :]
    sine = jnp.concatenate([jnp.sin(angles), jnp.sin(angles)], axis=1)[:, None, :]
    return (cosine, sine)


def causal_mask():
    counter = jnp.arange(SEQ, dtype=jnp.int32)
    return counter[:, None] >= counter[None, :]


def dot_full(left, right):
    return jnp.dot(left, right, precision=lax.Precision.HIGHEST, preferred_element_type=jnp.float32)


def attend_forward(query, keys, values):
    scores = (
        jnp.einsum("sqkgd,stkd->skgqt", query, keys, preferred_element_type=jnp.float32)
        * SCORE_SCALE
    )
    scores = jnp.where(causal_mask(), scores, NEG_LARGE)
    highest = jnp.max(scores, axis=-1, keepdims=True)
    weights = jnp.exp(scores - highest)
    totals = jnp.sum(weights, axis=-1, keepdims=True)
    log_total = highest + jnp.log(totals)
    probability = (weights / totals).astype(jnp.bfloat16)
    attended = jnp.einsum(
        "skgqt,stkd->sqkgd", probability, values, preferred_element_type=jnp.float32
    )
    return (attended.astype(jnp.bfloat16), log_total)


def attend_backward(query, keys, values, attended, log_total, grad_out):
    scores = (
        jnp.einsum("sqkgd,stkd->skgqt", query, keys, preferred_element_type=jnp.float32)
        * SCORE_SCALE
    )
    scores = jnp.where(causal_mask(), scores, NEG_LARGE)
    probability = jnp.exp(scores - log_total)
    value_grad = jnp.einsum(
        "skgqt,sqkgd->stkd",
        probability.astype(jnp.bfloat16),
        grad_out,
        preferred_element_type=jnp.float32,
    )
    prob_grad = jnp.einsum(
        "sqkgd,stkd->skgqt", grad_out, values, preferred_element_type=jnp.float32
    )
    delta_rows = jnp.sum(grad_out.astype(jnp.float32) * attended.astype(jnp.float32), axis=-1)
    delta_rows = jnp.transpose(delta_rows, (0, 2, 3, 1))[..., None]
    score_grad = (probability * (prob_grad - delta_rows)).astype(jnp.bfloat16)
    query_grad = (
        jnp.einsum("skgqt,stkd->sqkgd", score_grad, keys, preferred_element_type=jnp.float32)
        * SCORE_SCALE
    )
    key_grad = (
        jnp.einsum("skgqt,sqkgd->stkd", score_grad, query, preferred_element_type=jnp.float32)
        * SCORE_SCALE
    )
    return (query_grad, key_grad, value_grad)


MESH = pl.DeviceIdType.MESH


class Refs:
    def __init__(self, named):
        self.__dict__.update(named)

    def get(self, name):
        return self.__dict__[name]


def remote(source, target, send_sem, recv_sem, device):
    return pltpu.make_async_remote_copy(
        src_ref=source,
        dst_ref=target,
        send_sem=send_sem,
        recv_sem=recv_sem,
        device_id=device,
        device_id_type=MESH,
    )


class Link:
    def __init__(self, n, t):
        self.n, self.t, self.minor, self.half = n, t, n // 4, n // 2
        self.me, self.z = lax.axis_index("dp"), lax.axis_index("tensor")
        self.core, self.chip = lax.rem(self.me, 2), lax.div(self.me, 2)
        self.a, self.b = lax.div(self.chip, self.minor), lax.rem(self.chip, self.minor)
        self.partner = (self.me + 1 - 2 * self.core, self.z)
        self.across = (2 * self.dest(1, 0) + self.core, self.z)
        self.beside = [(2 * self.dest(0, j) + self.core, self.z) for j in range(1, self.minor)]
        self.line = [(self.me, lax.rem(self.z + d, t)) for d in range(1, t)]

    def dest(self, k, j):
        return lax.rem(self.a + k, 2) * self.minor + lax.rem(self.b + j, self.minor)

    def behind(self, k, j):
        return self.dest(k, self.minor - j)

    def greet(self, plane):
        barrier = pltpu.get_barrier_semaphore()
        peers = self.line + ([self.partner, self.across] + self.beside if plane else [])
        for device in peers:
            pl.semaphore_signal(barrier, inc=1, device_id=device, device_id_type=MESH)
        pl.semaphore_wait(barrier, len(peers))

    def nearest(self, i):
        z, t = self.z, self.t
        low = jnp.minimum(z, t - 1 - z)
        near = z - (i + 1) // 2 if i % 2 else z + i // 2
        far = jnp.where(2 * z < t, i, t - 1 - i)
        return jnp.where(i <= 2 * low, near, far)


def sum_line(link, part, slots, send_sem, recv_sem, rows, chunk):
    t, copies = link.t, {}
    for c in range(rows // chunk):
        for d in range(1, t):
            here = pl.ds(c * chunk, chunk)
            copies[c, d] = remote(
                part.at[lax.rem(link.z + d, t), here],
                slots.at[d - 1, here],
                send_sem.at[d - 1, c],
                recv_sem.at[d - 1, c],
                link.line[d - 1],
            )
            copies[c, d].start()

    def total(c):
        here = pl.ds(c * chunk, chunk)
        value = part[link.z, here].astype(jnp.float32)
        for d in range(1, t):
            copies[c, d].wait_recv()
            value = value + slots[d - 1, here].astype(jnp.float32)
        return value

    return total, list(copies.values())


def share_line(link, place, send_sem, recv_sem):
    copies = [
        remote(place, place, send_sem.at[d - 1], recv_sem.at[d - 1], link.line[d - 1])
        for d in range(1, link.t)
    ]
    for copy in copies:
        copy.start()
    return copies


def line_kernel(n, t, rows, chunk, finish, names, *refs):
    r = Refs(zip(names, refs))
    link = Link(n, t)
    link.greet(False)
    total, sent = sum_line(link, r.part, r.pre, r.pre_s, r.pre_r, rows, chunk)
    arriving = []
    for c in range(rows // chunk):
        here = pl.ds(c * chunk, chunk)
        r.shared[link.z, here] = finish(c, here, total(c), r)
        arriving += share_line(
            link, r.shared.at[link.z, here], r.post_s.at[c], r.post_r.at[c]
        )
    for copy in arriving:
        copy.wait_recv()
    for copy in sent + arriving:
        copy.wait_send()


def dot_nt(left, right):
    return lax.dot_general(
        left, right, (((1,), (1,)), ((), ())), preferred_element_type=jnp.float32
    )


def dot_nn(left, right):
    return jnp.dot(left, right, preferred_element_type=jnp.float32)


def dot_split(left, right):
    high = left.astype(jnp.bfloat16)
    low = (left - high.astype(jnp.float32)).astype(jnp.bfloat16)
    return dot_nn(high, right) + dot_nn(low, right)


def softmax_rows(logits):
    weights = jnp.exp(logits - jnp.max(logits, axis=1, keepdims=True))
    return weights / jnp.sum(weights, axis=1, keepdims=True)


def moe_kernel(n, t, rows, chunk, forward, backward, before, after, names, *refs):
    r = Refs(zip(names, refs))
    link = Link(n, t)
    me, z, core, minor, half = link.me, link.z, link.core, link.minor, link.half
    chunks = rows // chunk
    pieces = [(i, c) for i in range(t) for c in range(chunks)]
    gathered = r.gathered
    tokens = r.tokens if hasattr(r, "tokens") else gathered
    grads = r.grads if hasattr(r, "grads") else gathered
    width = gathered.shape[-1]
    link.greet(True)
    sent, kept = [], {}

    def go(key, *copy):
        kept[key] = remote(*copy)
        kept[key].start()
        sent.append(kept[key])

    total, copies = sum_line(link, r.part, r.pre, r.pre_s, r.pre_r, rows, chunk)
    sent.extend(copies)

    def slab(c):
        return pl.ds(c * chunk, chunk)

    def block(chip, p):
        i, c = pieces[p]
        return gathered.at[2 * chip + core, link.nearest(i), slab(c)]

    def acquire(p):
        i, c = pieces[p]
        if i == 0:
            mine = gathered.at[me, z, slab(c)]
            mine[...] = before(c, slab(c), total(c), r)
            sent.extend(share_line(link, mine, r.zg_s.at[c], r.zg_r.at[c]))
        else:
            s = link.nearest(i)
            slot = lax.rem(z - s + t, t) - 1
            place = gathered.at[me, s, slab(c)]
            remote(
                place, place, r.zg_s.at[c, slot], r.zg_r.at[c, slot], link.line[0]
            ).wait_recv()

    def to_partner(slot, chip, p):
        place = block(chip, p)
        go(("p", p, slot), place, place, r.p_s.at[p, slot], r.p_r.at[p, slot], link.partner)

    def stage_one(p):
        acquire(p)
        place = block(link.chip, p)
        go(("a", p), place, place, r.a_s.at[p], r.a_r.at[p], link.across)
        for j in range(1, minor):
            sems = r.b_s.at[p, j - 1], r.b_r.at[p, j - 1]
            go(("b", p, j), place, place, *sems, link.beside[j - 1])
        to_partner(0, link.chip, p)

    def stage_two(p):
        other = link.dest(1, 0)
        kept["a", p].wait_recv()
        if p % 2 == 0:
            for j in range(1, minor):
                place = block(other, p)
                sems = r.d_s.at[p, j - 1], r.d_r.at[p, j - 1]
                go(("d", p, j), place, place, *sems, link.beside[j - 1])
        to_partner(1, other, p)
        for j in range(1, minor):
            kept["b", p, j].wait_recv()
            if p % 2:
                place = block(link.behind(0, j), p)
                sems = r.d_s.at[p, j - 1], r.d_r.at[p, j - 1]
                go(("d", p, j), place, place, *sems, link.across)
            to_partner(1 + j, link.behind(0, j), p)

    def stage_three(p):
        for j in range(1, minor):
            kept["d", p, j].wait_recv()
            to_partner(minor + j, link.behind(1, j), p)

    order = [(k, j) for k in range(2) for j in range(minor)]

    def compute(p):
        i, c = pieces[p]
        for slot in range(half):
            kept["p", p, slot].wait_recv()
        s = link.nearest(i)
        places = [2 * link.dest(k, j) + 1 - core for k, j in order]
        places += [2 * link.dest(k, j) + core for k, j in order]

        def rows_of(ref):
            return jnp.concatenate([ref[place, s, slab(c)] for place in places], axis=0)

        def keep(name, value):
            for at, place in enumerate(places):
                r.get(name)[place, s, slab(c)] = value[at * chunk : (at + 1) * chunk]

        turn = late.index(p)
        if turn >= 2:
            kept["o", late[turn - 2]].wait_send()

        def put(value, low):
            value = value.astype(jnp.bfloat16)
            here = pl.ds(low, value.shape[1])
            for at, (k, j) in enumerate(order):
                r.outbox[turn % 2, k, j, :, here] = value[at * chunk : (at + 1) * chunk]
                own = value[(half + at) * chunk : (half + at + 1) * chunk]
                r.paired[p, k, j, :, here] = own

        x = rows_of(tokens)
        share = softmax_rows(dot_nn(x, r.router[...]))
        share = share * rows_of(r.chosen)[:, :EXPERTS].astype(jnp.float32)
        weights = dot_split(share, r.select[...])
        gate_pre = dot_nt(x, r.gate[...])
        up_pre = dot_nt(x, r.up[...])
        sigma = jax.nn.sigmoid(gate_pre)
        silu = gate_pre * sigma
        activated = silu * up_pre
        low = 0
        if forward or backward:
            weighted = (weights * activated).astype(jnp.bfloat16)
        if backward:
            keep("weighted", weighted)
            back = dot_nt(rows_of(grads), r.down[...])
            put(dot_split(activated * back, r.gather[...]), width)
            act_grad = weights * back
            gate_rows = act_grad * up_pre * sigma * (1.0 + gate_pre * (1.0 - sigma))
            gate_rows = gate_rows.astype(jnp.bfloat16)
            up_rows = (act_grad * silu).astype(jnp.bfloat16)
            keep("gate_rows", gate_rows)
            keep("up_rows", up_rows)
            put(dot_nn(gate_rows, r.gate[...]) + dot_nn(up_rows, r.up[...]), 0)
            low = width + 128
        if forward:
            put(dot_nn(weighted, r.down[...]), low)
        kept["o", p] = remote(
            r.outbox.at[turn % 2], r.pairs.at[p], r.o_s.at[p], r.o_r.at[p], link.partner
        )
        kept["o", p].start()

    def rs_one(p):
        kept["o", p].wait_recv()
        value = r.paired[p].astype(jnp.float32) + r.pairs[p].astype(jnp.float32)
        r.paired[p] = value.astype(jnp.bfloat16)
        q = p // 2
        if p % 2 == 0:
            sems = r.fa_s.at[q], r.fa_r.at[q]
            go(("f", p), r.paired.at[p, 1], r.first_a.at[q], *sems, link.across)
        else:
            for j in range(1, minor):
                sems = r.fb_s.at[q, j - 1], r.fb_r.at[q, j - 1]
                source, target = r.paired.at[p, :, j], r.first_b.at[q, j - 1]
                go(("f", p, j), source, target, *sems, link.beside[j - 1])

    def rs_two(p):
        q = p // 2
        if p % 2 == 0:
            kept["f", p].wait_recv()
            value = r.paired[p, 0].astype(jnp.float32) + r.first_a[q].astype(jnp.float32)
            r.paired[p, 0] = value.astype(jnp.bfloat16)
            for j in range(1, minor):
                sems = r.sb_s.at[q, j - 1], r.sb_r.at[q, j - 1]
                source, target = r.paired.at[p, 0, j], r.second_b.at[q, j - 1]
                go(("s", p, j), source, target, *sems, link.beside[j - 1])
        else:
            value = r.paired[p, :, 0].astype(jnp.float32)
            for j in range(1, minor):
                kept["f", p, j].wait_recv()
                value = value + r.first_b[q, j - 1].astype(jnp.float32)
            r.paired[p, :, 0] = value.astype(jnp.bfloat16)
            sems = r.sa_s.at[q], r.sa_r.at[q]
            go(("s", p), r.paired.at[p, 1, 0], r.second_a.at[q], *sems, link.across)

    def rs_three(p):
        i, c = pieces[p]
        q = p // 2
        value = r.paired[p, 0, 0].astype(jnp.float32)
        if p % 2 == 0:
            for j in range(1, minor):
                kept["s", p, j].wait_recv()
                value = value + r.second_b[q, j - 1].astype(jnp.float32)
        else:
            kept["s", p].wait_recv()
            value = value + r.second_a[q].astype(jnp.float32)
        r.total[p] = value.astype(jnp.bfloat16)
        if i:
            s = link.nearest(i)
            slot = lax.rem(s - z + t, t) - 1
            go(
                ("z", p),
                r.total.at[p],
                r.last.at[slot, c],
                r.last_s.at[slot, c],
                r.last_r.at[slot, c],
                (me, s),
            )

    arriving = []

    def rs_four(p):
        i, c = pieces[p]
        if i:
            return
        value = r.total[p].astype(jnp.float32)
        for d in range(1, t):
            remote(
                r.total.at[p],
                r.last.at[d - 1, c],
                r.last_s.at[d - 1, c],
                r.last_r.at[d - 1, c],
                link.line[d - 1],
            ).wait_recv()
            value = value + r.last[d - 1, c].astype(jnp.float32)
        for at, result in enumerate(after(c, slab(c), value, r)):
            target = r.get("shared%d" % at).at[z, slab(c)]
            target[...] = result
            arriving.extend(share_line(link, target, r.post_s.at[at, c], r.post_r.at[at, c]))

    late = list(range(chunks, len(pieces))) + list(range(chunks))
    numbers = list(range(len(pieces)))
    skip = min(chunks, len(pieces) - chunks)
    schedule = [(0, stage_one, numbers), (2, stage_two, numbers), (4, stage_three, numbers)]
    schedule += [(10 + skip, rs_three, late), (10 + skip, rs_four, late), (8 + skip, rs_two, late)]
    schedule += [(6 + skip, rs_one, late), (4 + skip, compute, late)]
    for step in range(len(pieces) + 10 + skip):
        for lag, stage, which in schedule:
            if 0 <= step - lag < len(pieces):
                stage(which[step - lag])

    for copy in arriving:
        copy.wait_recv()
    for copy in sent + arriving:
        copy.wait_send()
    for p in late[-2:]:
        kept["o", p].wait_send()


def call(kernel, operands, results, scratch, collective_id):
    vmem = pl.BlockSpec(memory_space=pltpu.VMEM)
    found = pl.pallas_call(
        functools.partial(kernel, list(operands) + list(results) + list(scratch)),
        out_shape=list(results.values()),
        in_specs=[vmem] * len(operands),
        out_specs=[vmem] * len(results),
        scratch_shapes=list(scratch.values()),
        compiler_params=pltpu.CompilerParams(
            collective_id=collective_id, has_side_effects=True, vmem_limit_bytes=56 * 2**20
        ),
    )(*operands.values())
    return dict(zip(results, found))


def both(name, *shape):
    sems = pltpu.SemaphoreType.DMA(shape)
    return {name + "_s": sems, name + "_r": sems}


def bf16(*shape):
    return jax.ShapeDtypeStruct(shape, jnp.bfloat16)


def f32(*shape):
    return jax.ShapeDtypeStruct(shape, jnp.float32)


def line_call(part, operands, results, finish, chunk, collective_id):
    n, t = lax.axis_size("dp"), lax.axis_size("tensor")
    rows, width = part.shape[0] // t, part.shape[1]
    chunk = min(chunk, rows)
    chunks = rows // chunk
    scratch = dict(pre=pltpu.VMEM((t - 1, rows, width), jnp.bfloat16))
    scratch |= both("pre", t - 1, chunks) | both("post", chunks, t - 1)
    kernel = lambda names, *refs: line_kernel(n, t, rows, chunk, finish, names, *refs)
    operands = dict(part=part.reshape(t, rows, width)) | operands
    results = dict(shared=bf16(t, rows, width)) | results
    return call(kernel, operands, results, scratch, collective_id)


def moe_call(
    part, operands, results, before, after, forward, backward, shared, chunk, collective_id
):
    n, t = lax.axis_size("dp"), lax.axis_size("tensor")
    rows, width = part.shape[0] // t, part.shape[1]
    chunk = min(chunk, rows)
    chunks, half, minor = rows // chunk, n // 2, n // 4
    count = t * chunks
    even, odd = (count + 1) // 2, max(count // 2, 1)
    total = (width if forward else 0) + (width + 128 if backward else 0)
    hidden = operands["gate"].shape[0]
    slots = lambda *lead: pltpu.VMEM(lead + (chunk, total), jnp.bfloat16)
    scratch = dict(
        pre=pltpu.VMEM((t - 1, rows, width), jnp.bfloat16),
        outbox=slots(2, 2, minor),
        paired=slots(count, 2, minor),
        pairs=slots(count, 2, minor),
        first_a=slots(even, minor),
        first_b=slots(odd, minor - 1, 2),
        second_a=slots(odd),
        second_b=slots(even, minor - 1),
        total=slots(count),
        last=slots(t - 1, chunks),
    )
    scratch |= both("pre", t - 1, chunks) | both("zg", chunks, t - 1) | both("p", count, half)
    scratch |= both("a", count) | both("b", count, minor - 1) | both("d", count, minor - 1)
    scratch |= both("o", count) | both("fa", even) | both("fb", odd, minor - 1)
    scratch |= both("sa", odd) | both("sb", even, minor - 1) | both("last", t - 1, chunks)
    scratch |= both("post", shared, chunks, t - 1)
    everywhere = lambda depth: bf16(n, t, rows, depth)
    found = dict(gathered=everywhere(width))
    if backward:
        found |= {name: everywhere(hidden) for name in ("weighted", "gate_rows", "up_rows")}
    found |= {"shared%d" % at: bf16(t, rows, width) for at in range(shared)}
    kernel = lambda names, *refs: moe_kernel(
        n, t, rows, chunk, forward, backward, before, after, names, *refs
    )
    operands = dict(part=part.reshape(t, rows, width)) | operands
    return call(kernel, operands, found | results, scratch, collective_id)


def spread_kernel(n, t, names, *refs):
    r = Refs(zip(names, refs))
    link = Link(n, t)
    me = link.me
    others = [(lax.rem(me + d, n), link.z) for d in range(1, n)]
    barrier = pltpu.get_barrier_semaphore()
    for device in link.line + others:
        pl.semaphore_signal(barrier, inc=1, device_id=device, device_id_type=MESH)
    pl.semaphore_wait(barrier, len(link.line) + len(others))
    copies = []
    for d, device in enumerate(link.line):
        copies.append(remote(r.gain, r.gains.at[d], r.g_s.at[d], r.g_r.at[d], device))
        copies.append(remote(r.side, r.sides.at[d], r.d_s.at[d], r.d_r.at[d], device))
    for copy in copies:
        copy.start()
    value = r.gain[...]
    for d in range(t - 1):
        copies[2 * d].wait_recv()
        value = value + r.gains[d]
    r.summed[...] = value
    outward = []
    for d, device in enumerate(others):
        source = r.summed.at[device[0]]
        outward.append(remote(source, r.slices.at[d], r.o_s.at[d], r.o_r.at[d], device))
        outward[-1].start()
    value = r.side[...]
    for d in range(t - 1):
        copies[2 * d + 1].wait_recv()
        value = value + r.sides[d]
    r.side_out[...] = value
    value = r.summed[me]
    for d in range(n - 1):
        outward[d].wait_recv()
        value = value + r.slices[d]
    r.gain_out[...] = value
    for copy in copies + outward:
        copy.wait_send()


def spread_call(side, gain, collective_id):
    n, t = lax.axis_size("dp"), lax.axis_size("tensor")
    width = gain.shape[1] // n
    gain = jnp.broadcast_to(gain.reshape(n, 1, width), (n, 8, width))
    vmem = lambda *shape: pltpu.VMEM(shape, jnp.float32)
    scratch = dict(
        gains=vmem(t - 1, n, 8, width),
        sides=vmem(t - 1, *side.shape),
        summed=vmem(n, 8, width),
        slices=vmem(n - 1, 8, width),
    )
    scratch |= both("g", t - 1) | both("d", t - 1) | both("o", n - 1)
    results = dict(side_out=f32(*side.shape), gain_out=f32(8, width))
    kernel = lambda names, *refs: spread_kernel(n, t, names, *refs)
    found = call(kernel, dict(side=side, gain=gain), results, scratch, collective_id)
    return found["side_out"], found["gain_out"][0]


def row_norm(source, gain):
    scale = lax.rsqrt(jnp.mean(source * source, axis=1, keepdims=True) + EPSILON)
    return scale, source * scale * gain


def row_norm_backward(grad_in, source, gain):
    scale = lax.rsqrt(jnp.mean(source * source, axis=1, keepdims=True) + EPSILON)
    gain_grad = jnp.sum(grad_in * source * scale, axis=0, keepdims=True)
    scaled = grad_in * gain
    inner = jnp.mean(scaled * source, axis=1, keepdims=True)
    return scale * (scaled - source * scale * scale * inner), gain_grad


def add_up(c, ref, value):
    ref[...] = value if c == 0 else ref[...] + value


def attention_done(c, here, value, r):
    middle = r.inputs[here] + RESIDUAL_SCALE * value
    r.middle[here] = middle
    return row_norm(middle, r.mixture_gain[...])[1].astype(jnp.bfloat16)


def layer_done(c, here, value, r):
    output = r.middle[here] + RESIDUAL_SCALE * value
    r.output[here] = output
    return (row_norm(output, r.next_gain[...])[1].astype(jnp.bfloat16),)


def mixture_backward_done(c, here, value, r):
    width, count = r.middle.shape[1], r.router.shape[1]
    link_me, z = lax.axis_index("dp"), lax.axis_index("tensor")
    tokens = r.tokens if hasattr(r, "tokens") else r.gathered
    share = softmax_rows(dot_nn(tokens[link_me, z, here], r.router[...]))
    prob_grad = r.chosen[link_me, z, here][:, :EXPERTS].astype(jnp.float32) * value[:, width : width + count]
    logit_grad = share * (prob_grad - jnp.sum(share * prob_grad, axis=1, keepdims=True))
    second_grad = value[:, :width] + dot_full(logit_grad, r.router_t[...])
    middle = r.middle[here]
    norm_grad, gain_grad = row_norm_backward(second_grad, middle, r.mixture_gain[...])
    grad_out = r.grad if hasattr(r, "grad") else r.grad_out
    middle_grad = grad_out[here] + norm_grad
    r.middle_grad[here] = middle_grad
    r.logit_grad[here] = logit_grad
    add_up(c, r.mixture_gain_grad, gain_grad)
    results = ((RESIDUAL_SCALE * middle_grad).astype(jnp.bfloat16),)
    if value.shape[1] > width + 128:
        last = middle + RESIDUAL_SCALE * value[:, width + 128 :]
        results += (last.astype(jnp.bfloat16),)
    return results


def attention_backward_done(scale, c, here, value, r):
    norm_grad, gain_grad = row_norm_backward(value, r.inputs[here], r.attention_gain[...])
    grad = r.upper_grad[here] + norm_grad
    r.grad[here] = grad
    add_up(c, r.attention_gain_grad, gain_grad)
    return (scale * grad).astype(jnp.bfloat16)


def own_rows(array, offset=0):
    rows = SEQ // lax.axis_size("tensor")
    return lax.dynamic_slice_in_dim(array, offset + lax.axis_index("tensor") * rows, rows, axis=0)


def attention_forward(first_input, params, cosine, sine):
    query_weight, key_weight, value_weight, output_weight = params[1:5]
    row_count = first_input.shape[0]
    query_heads = query_weight.shape[1] // HD
    key_heads = key_weight.shape[0] // HD
    group_size = query_heads // key_heads
    seq_count = row_count // SEQ
    query = jnp.dot(first_input, query_weight, preferred_element_type=jnp.float32).reshape(
        row_count, query_heads, HD
    )
    keys = jnp.dot(first_input, key_weight.T, preferred_element_type=jnp.float32).reshape(
        row_count, key_heads, HD
    )
    values = jnp.dot(first_input, value_weight.T, preferred_element_type=jnp.float32).astype(
        jnp.bfloat16
    )
    query = (query * cosine + rotate_half(query) * sine).astype(jnp.bfloat16)
    keys = (keys * cosine + rotate_half(keys) * sine).astype(jnp.bfloat16)
    query_split = query.reshape(seq_count, SEQ, key_heads, group_size, HD)
    key_split = keys.reshape(seq_count, SEQ, key_heads, HD)
    value_split = values.reshape(seq_count, SEQ, key_heads, HD)
    attended, log_total = attend_forward(query_split, key_split, value_split)
    attended_rows = attended.reshape(row_count, query_heads * HD)
    part = jnp.dot(attended_rows, output_weight, preferred_element_type=jnp.float32)
    return part.astype(jnp.bfloat16), (query_split, key_split, value_split, attended, log_total)


def attention_backward(attention_grad, first_input, saved, params, cosine, sine):
    query_weight, key_weight, value_weight, output_weight = params[1:5]
    query_split, key_split, value_split, attended, log_total = saved
    row_count, width = attention_grad.shape
    query_heads = query_weight.shape[1] // HD
    key_heads = key_weight.shape[0] // HD
    attended_rows = attended.reshape(row_count, query_heads * HD)
    output_grad = jnp.dot(attention_grad.T, attended_rows, preferred_element_type=jnp.float32)
    attended_grad = jnp.dot(
        attention_grad, output_weight.T, preferred_element_type=jnp.float32
    ).astype(jnp.bfloat16)
    query_grad, key_grad, value_grad = attend_backward(
        query_split,
        key_split,
        value_split,
        attended,
        log_total,
        attended_grad.reshape(attended.shape),
    )
    query_grad = query_grad.reshape(row_count, query_heads, HD)
    query_grad = (
        (query_grad * cosine - rotate_half(query_grad) * sine)
        .astype(jnp.bfloat16)
        .reshape(row_count, query_heads * HD)
    )
    key_grad = key_grad.reshape(row_count, key_heads, HD)
    key_grad = (
        (key_grad * cosine - rotate_half(key_grad) * sine)
        .astype(jnp.bfloat16)
        .reshape(row_count, key_heads * HD)
    )
    value_grad = value_grad.astype(jnp.bfloat16).reshape(row_count, key_heads * HD)
    first_part = (
        jnp.dot(query_grad, query_weight.T, preferred_element_type=jnp.float32)
        + jnp.dot(key_grad, key_weight, preferred_element_type=jnp.float32)
        + jnp.dot(value_grad, value_weight, preferred_element_type=jnp.float32)
    ).astype(jnp.bfloat16)
    projected = jnp.dot(
        first_input.T,
        jnp.concatenate([query_grad, key_grad, value_grad], axis=1),
        preferred_element_type=jnp.float32,
    )
    return first_part, jnp.concatenate([projected, output_grad], axis=1)


def shards(
    hidden_states,
    output_cotangent,
    routes,
    attention_gain,
    query_weight,
    key_weight,
    value_weight,
    output_weight,
    mixture_gain,
    router_weight,
    gate_weight,
    up_weight,
    down_weight,
):
    params_all = (
        attention_gain,
        query_weight,
        key_weight,
        value_weight,
        output_weight,
        mixture_gain,
        router_weight,
        gate_weight,
        up_weight,
        down_weight,
    )
    n, t = lax.axis_size("dp"), lax.axis_size("tensor")
    row_count, width = hidden_states.shape
    rows = row_count // t
    layer_count = query_weight.shape[0]
    cosine, sine = rope_tables(row_count)
    local_experts, hidden = gate_weight.shape[1:3]
    expert_ids = jnp.arange(EXPERTS, dtype=jnp.int32)
    chosen = jnp.any(routes[:, :, None] == expert_ids[None, None, :], axis=1)
    first = (RESIDUAL_SCALE * output_cotangent).astype(jnp.bfloat16)
    side = jnp.pad(chosen.astype(jnp.bfloat16), ((0, 0), (0, 128 - EXPERTS)))
    chosen_all = lax.all_gather(side, "dp", axis=0, tiled=True)
    first, chosen_all = lax.optimization_barrier((first, chosen_all))
    cotangents = lax.all_gather(first, "dp", axis=0, tiled=True)
    everywhere = lambda array: array.reshape(n, t, rows, array.shape[-1])
    owners = lax.axis_index("dp") * local_experts + jnp.arange(local_experts * hidden) // hidden
    select = (expert_ids[:, None] == owners[None, :]).astype(jnp.bfloat16)
    gather = jnp.pad(select.T, ((0, 0), (0, 128 - EXPERTS)))
    params = [tuple(weight[i] for weight in params_all) for i in range(layer_count)]
    gains = lambda i, kind: params[i][kind][None, :]
    chosen_all = everywhere(chosen_all)

    def shared_operands(i):
        flat = lambda array: array.reshape(local_experts * hidden, width)
        return dict(
            router=params[i][6],
            gate=flat(params[i][7]),
            up=flat(params[i][8]),
            down=flat(params[i][9]),
            select=select,
            gather=gather,
            chosen=chosen_all,
        )

    first_input = row_norm(hidden_states, gains(0, 0))[1].astype(jnp.bfloat16)
    current = own_rows(hidden_states)
    kept = []
    backward_operands = lambda i: dict(
        router_t=params[i][6].astype(jnp.float32).T,
        mixture_gain=gains(i, 5),
    )
    backward_results = dict(
        middle_grad=f32(rows, width),
        logit_grad=f32(rows, EXPERTS),
        mixture_gain_grad=f32(1, width),
    )
    for i in range(layer_count):
        part, heads = attention_forward(first_input, params[i], cosine, sine)
        operands = shared_operands(i) | dict(inputs=current, mixture_gain=gains(i, 5))
        results = dict(middle=f32(rows, width))
        if i + 1 < layer_count:
            found = moe_call(
                part,
                operands | dict(next_gain=gains(i + 1, 0)),
                results | dict(output=f32(rows, width)),
                attention_done,
                layer_done,
                True,
                False,
                1,
                32,
                1 + i,
            )
            kept.append((first_input, current, heads, found))
            first_input = found["shared0"].reshape(row_count, width)
            current = found["output"]
        else:
            found = moe_call(
                part,
                operands
                | backward_operands(i)
                | dict(
                    grads=everywhere(cotangents),
                    grad_out=own_rows(output_cotangent),
                ),
                results | backward_results,
                attention_done,
                mixture_backward_done,
                True,
                True,
                2,
                32,
                1 + i,
            )
            kept.append((first_input, current, heads, found))
            last = found["shared1"].reshape(row_count, width)
    dense_layers = [None] * layer_count
    expert_layers = [None] * layer_count
    grads = everywhere(cotangents)
    for i in reversed(range(layer_count)):
        first_input, current, heads, ahead = kept[i]
        tokens = ahead["gathered"]
        if i + 1 < layer_count:
            found = moe_call(
                part,
                shared_operands(i)
                | backward_operands(i)
                | dict(
                    tokens=tokens,
                    middle=ahead["middle"],
                    inputs=upper_inputs,
                    attention_gain=gains(i + 1, 0),
                    upper_grad=found["middle_grad"],
                ),
                backward_results | dict(grad=f32(rows, width), attention_gain_grad=f32(1, width)),
                functools.partial(attention_backward_done, RESIDUAL_SCALE),
                mixture_backward_done,
                False,
                True,
                1,
                32,
                11 + i,
            )
            grads = found["gathered"]
            smalls[i + 1].append(found["attention_gain_grad"])
        else:
            found = ahead
            smalls = [None] * layer_count
        part, dense_layers[i] = attention_backward(
            found["shared0"].reshape(row_count, width), first_input, heads, params[i], cosine, sine
        )
        upper_inputs = current
        flat = lambda array: array.reshape(n * row_count, array.shape[-1])
        across = lambda left, right: lax.dot_general(
            flat(left), flat(right), (((0,), (0,)), ((), ())), preferred_element_type=jnp.float32
        ).reshape(local_experts, hidden, width)
        expert_layers[i] = (
            across(found["gate_rows"], tokens),
            across(found["up_rows"], tokens),
            across(found["weighted"], grads),
        )
        own_second = own_rows(flat(tokens), lax.axis_index("dp") * SEQ).astype(jnp.float32)
        smalls[i] = [dot_full(own_second.T, found["logit_grad"]), found["mixture_gain_grad"]]
    tail = line_call(
        part,
        dict(
            inputs=upper_inputs,
            attention_gain=gains(0, 0),
            upper_grad=found["middle_grad"],
        ),
        dict(grad=f32(rows, width), attention_gain_grad=f32(1, width)),
        functools.partial(attention_backward_done, 1.0),
        32,
        21,
    )
    sides = []
    for i in reversed(range(layer_count)):
        router_grad, mixture_gain_grad = smalls[i][:2]
        attention_gain_grad = smalls[i][2] if i else jnp.zeros((1, width), jnp.float32)
        small = jnp.concatenate(
            [
                router_grad,
                attention_gain_grad.T,
                mixture_gain_grad.T,
                jnp.zeros((width, 126 - EXPERTS), jnp.float32),
            ],
            axis=1,
        )
        dense = lax.psum_scatter(
            jnp.concatenate([dense_layers[i], small], axis=1).astype(jnp.bfloat16),
            "dp",
            scatter_dimension=0,
            tiled=True,
        ).astype(jnp.float32)
        sides = [dense[:, -128 : 40 - 128].T] + sides
        q, k = query_weight.shape[2], key_weight.shape[1]
        dense_layers[i] = (
            dense[:, :q],
            dense[:, q : q + k].T,
            dense[:, q + k : q + 2 * k].T,
            dense[:, q + 2 * k : 2 * q + 2 * k].T,
        )
    sides, first_gain = spread_call(
        jnp.concatenate(sides, axis=0), tail["attention_gain_grad"], 31
    )
    sides = sides.reshape(layer_count, 40, -1)
    attention_gains = jnp.concatenate([first_gain[None], sides[1:, EXPERTS]], axis=0)
    dense = [jnp.stack([entry[position] for entry in dense_layers]) for position in range(4)]
    stacked = [attention_gains, *dense, sides[:, EXPERTS + 1], sides[:, :EXPERTS].transpose(0, 2, 1)]
    stacked += [jnp.stack([entry[position] for entry in expert_layers]) for position in range(3)]
    result = tail["shared"].reshape(row_count, width)
    return (last.astype(jnp.float32), result.astype(jnp.float32), *stacked)


def solution(mesh):
    placed = (
        P("dp", None),
        P("dp", None),
        P("dp", None),
        P(),
        P(None, None, "tensor"),
        P(None, "tensor", None),
        P(None, "tensor", None),
        P(None, "tensor", None),
        P(),
        P(),
        P(None, "dp", "tensor", None),
        P(None, "dp", "tensor", None),
        P(None, "dp", "tensor", None),
    )
    return jax.shard_map(
        shards,
        mesh=mesh,
        in_specs=placed,
        out_specs=(
            P("dp", None),
            P("dp", None),
            P(None, "dp"),
            P(None, "dp", "tensor"),
            P(None, "tensor", "dp"),
            P(None, "tensor", "dp"),
            P(None, "tensor", "dp"),
            P(None, "dp"),
            P(None, "dp", None),
            P(None, "dp", "tensor", None),
            P(None, "dp", "tensor", None),
            P(None, "dp", "tensor", None),
        ),
        check_vma=False,
    )
```

```python
import functools

import jax
import jax.numpy as jnp
from jax import lax
from jax.experimental import pallas as pl
from jax.experimental.pallas import tpu as pltpu
from jax.sharding import PartitionSpec as P

HD = 64
EXPERTS = 32
SEQ = 256


EPSILON = 1e-06
RESIDUAL_SCALE = 0.22
SCORE_SCALE = 0.015625
ROPE_BASE = 10000.0
NEG_LARGE = -1e30


def rotate_half(values):
    middle = values.shape[-1] // 2
    return jnp.concatenate([-values[..., middle:], values[..., :middle]], axis=-1)


def rope_tables(row_count):
    middle = HD // 2
    positions = (jnp.arange(row_count, dtype=jnp.int32) % SEQ).astype(jnp.float32)
    inverse_rate = ROPE_BASE ** (
        -(jnp.arange(middle, dtype=jnp.int32).astype(jnp.float32) * (2.0 / HD))
    )
    angles = positions[:, None] * inverse_rate[None, :]
    cosine = jnp.concatenate([jnp.cos(angles), jnp.cos(angles)], axis=1)[:, None, :]
    sine = jnp.concatenate([jnp.sin(angles), jnp.sin(angles)], axis=1)[:, None, :]
    return (cosine, sine)


def causal_mask():
    counter = jnp.arange(SEQ, dtype=jnp.int32)
    return counter[:, None] >= counter[None, :]


def dot_full(left, right):
    return jnp.dot(left, right, precision=lax.Precision.HIGHEST, preferred_element_type=jnp.float32)


def attend_forward(query, keys, values):
    scores = (
        jnp.einsum("sqkgd,stkd->skgqt", query, keys, preferred_element_type=jnp.float32)
        * SCORE_SCALE
    )
    scores = jnp.where(causal_mask(), scores, NEG_LARGE)
    highest = jnp.max(scores, axis=-1, keepdims=True)
    weights = jnp.exp(scores - highest)
    totals = jnp.sum(weights, axis=-1, keepdims=True)
    log_total = highest + jnp.log(totals)
    probability = (weights / totals).astype(jnp.bfloat16)
    attended = jnp.einsum(
        "skgqt,stkd->sqkgd", probability, values, preferred_element_type=jnp.float32
    )
    return (attended.astype(jnp.bfloat16), log_total)


def attend_backward(query, keys, values, attended, log_total, grad_out):
    scores = (
        jnp.einsum("sqkgd,stkd->skgqt", query, keys, preferred_element_type=jnp.float32)
        * SCORE_SCALE
    )
    scores = jnp.where(causal_mask(), scores, NEG_LARGE)
    probability = jnp.exp(scores - log_total)
    value_grad = jnp.einsum(
        "skgqt,sqkgd->stkd",
        probability.astype(jnp.bfloat16),
        grad_out,
        preferred_element_type=jnp.float32,
    )
    prob_grad = jnp.einsum(
        "sqkgd,stkd->skgqt", grad_out, values, preferred_element_type=jnp.float32
    )
    delta_rows = jnp.sum(grad_out.astype(jnp.float32) * attended.astype(jnp.float32), axis=-1)
    delta_rows = jnp.transpose(delta_rows, (0, 2, 3, 1))[..., None]
    score_grad = (probability * (prob_grad - delta_rows)).astype(jnp.bfloat16)
    query_grad = (
        jnp.einsum("skgqt,stkd->sqkgd", score_grad, keys, preferred_element_type=jnp.float32)
        * SCORE_SCALE
    )
    key_grad = (
        jnp.einsum("skgqt,sqkgd->stkd", score_grad, query, preferred_element_type=jnp.float32)
        * SCORE_SCALE
    )
    return (query_grad, key_grad, value_grad)


MESH = pl.DeviceIdType.MESH


class Refs:
    def __init__(self, named):
        self.__dict__.update(named)

    def get(self, name):
        return self.__dict__[name]


def remote(source, target, send_sem, recv_sem, device):
    return pltpu.make_async_remote_copy(
        src_ref=source,
        dst_ref=target,
        send_sem=send_sem,
        recv_sem=recv_sem,
        device_id=device,
        device_id_type=MESH,
    )


class Link:
    def __init__(self, n, t):
        self.n, self.t, self.minor, self.half = n, t, n // 4, n // 2
        self.me, self.z = lax.axis_index("dp"), lax.axis_index("tensor")
        self.core, self.chip = lax.rem(self.me, 2), lax.div(self.me, 2)
        self.a, self.b = lax.div(self.chip, self.minor), lax.rem(self.chip, self.minor)
        self.partner = (self.me + 1 - 2 * self.core, self.z)
        self.across = (2 * self.dest(1, 0) + self.core, self.z)
        self.beside = [(2 * self.dest(0, j) + self.core, self.z) for j in range(1, self.minor)]
        self.line = [(self.me, lax.rem(self.z + d, t)) for d in range(1, t)]

    def dest(self, k, j):
        return lax.rem(self.a + k, 2) * self.minor + lax.rem(self.b + j, self.minor)

    def behind(self, k, j):
        return self.dest(k, self.minor - j)

    def greet(self, plane):
        barrier = pltpu.get_barrier_semaphore()
        peers = self.line + ([self.partner, self.across] + self.beside if plane else [])
        for device in peers:
            pl.semaphore_signal(barrier, inc=1, device_id=device, device_id_type=MESH)
        pl.semaphore_wait(barrier, len(peers))

    def nearest(self, i):
        z, t = self.z, self.t
        low = jnp.minimum(z, t - 1 - z)
        near = z - (i + 1) // 2 if i % 2 else z + i // 2
        far = jnp.where(2 * z < t, i, t - 1 - i)
        return jnp.where(i <= 2 * low, near, far)


def sum_line(link, part, slots, send_sem, recv_sem, rows, chunk):
    t, copies = link.t, {}
    for c in range(rows // chunk):
        for d in range(1, t):
            here = pl.ds(c * chunk, chunk)
            copies[c, d] = remote(
                part.at[lax.rem(link.z + d, t), here],
                slots.at[d - 1, here],
                send_sem.at[d - 1, c],
                recv_sem.at[d - 1, c],
                link.line[d - 1],
            )
            copies[c, d].start()

    def total(c):
        here = pl.ds(c * chunk, chunk)
        value = part[link.z, here].astype(jnp.float32)
        for d in range(1, t):
            copies[c, d].wait_recv()
            value = value + slots[d - 1, here].astype(jnp.float32)
        return value

    return total, list(copies.values())


def share_line(link, place, send_sem, recv_sem):
    copies = [
        remote(place, place, send_sem.at[d - 1], recv_sem.at[d - 1], link.line[d - 1])
        for d in range(1, link.t)
    ]
    for copy in copies:
        copy.start()
    return copies


def line_kernel(n, t, rows, chunk, finish, names, *refs):
    r = Refs(zip(names, refs))
    link = Link(n, t)
    others = [(lax.rem(link.me + d, n), link.z) for d in range(1, n)]
    barrier = pltpu.get_barrier_semaphore()
    for device in link.line + others:
        pl.semaphore_signal(barrier, inc=1, device_id=device, device_id_type=MESH)
    pl.semaphore_wait(barrier, len(link.line) + len(others))
    total, sent = sum_line(link, r.part, r.pre, r.pre_s, r.pre_r, rows, chunk)
    outward = [
        remote(r.dense.at[device[0]], r.slots.at[d], r.w_s.at[d], r.w_r.at[d], device)
        for d, device in enumerate(others)
    ]
    for copy in outward:
        copy.start()
    arriving = []
    for c in range(rows // chunk):
        here = pl.ds(c * chunk, chunk)
        r.shared[link.z, here] = finish(c, here, total(c), r)
        arriving += share_line(
            link, r.shared.at[link.z, here], r.post_s.at[c], r.post_r.at[c]
        )
    for copy in arriving:
        copy.wait_recv()
    value = r.dense[link.me].astype(jnp.float32)
    for d, copy in enumerate(outward):
        copy.wait_recv()
        value = value + r.slots[d].astype(jnp.float32)
    r.dense_out[...] = value
    for copy in sent + arriving + outward:
        copy.wait_send()


def dot_nt(left, right):
    return lax.dot_general(
        left, right, (((1,), (1,)), ((), ())), preferred_element_type=jnp.float32
    )


def dot_tn(left, right):
    return lax.dot_general(
        left, right, (((0,), (0,)), ((), ())), preferred_element_type=jnp.float32
    )


def dot_nn(left, right):
    return jnp.dot(left, right, preferred_element_type=jnp.float32)


def dot_split(left, right):
    high = left.astype(jnp.bfloat16)
    low = (left - high.astype(jnp.float32)).astype(jnp.bfloat16)
    return dot_nn(high, right) + dot_nn(low, right)


def softmax_rows(logits):
    weights = jnp.exp(logits - jnp.max(logits, axis=1, keepdims=True))
    return weights / jnp.sum(weights, axis=1, keepdims=True)


def moe_kernel(n, t, rows, chunk, forward, backward, before, after, names, *refs):
    r = Refs(zip(names, refs))
    link = Link(n, t)
    me, z, core, minor, half = link.me, link.z, link.core, link.minor, link.half
    chunks = rows // chunk
    pieces = [(i, c) for i in range(t) for c in range(chunks)]
    gathered = r.gathered
    tokens = r.tokens if hasattr(r, "tokens") else gathered
    grads = r.grads if hasattr(r, "grads") else gathered
    width = gathered.shape[-1]
    link.greet(True)
    sent, kept = [], {}

    def go(key, *copy):
        kept[key] = remote(*copy)
        kept[key].start()
        sent.append(kept[key])

    total, copies = sum_line(link, r.part, r.pre, r.pre_s, r.pre_r, rows, chunk)
    sent.extend(copies)

    def slab(c):
        return pl.ds(c * chunk, chunk)

    def block(chip, p):
        i, c = pieces[p]
        return gathered.at[2 * chip + core, link.nearest(i), slab(c)]

    def acquire(p):
        i, c = pieces[p]
        if i == 0:
            mine = gathered.at[me, z, slab(c)]
            mine[...] = before(c, slab(c), total(c), r)
            sent.extend(share_line(link, mine, r.zg_s.at[c], r.zg_r.at[c]))
        else:
            s = link.nearest(i)
            slot = lax.rem(z - s + t, t) - 1
            place = gathered.at[me, s, slab(c)]
            remote(
                place, place, r.zg_s.at[c, slot], r.zg_r.at[c, slot], link.line[0]
            ).wait_recv()

    def to_partner(slot, chip, p):
        place = block(chip, p)
        go(("p", p, slot), place, place, r.p_s.at[p, slot], r.p_r.at[p, slot], link.partner)

    def stage_one(p):
        acquire(p)
        place = block(link.chip, p)
        go(("a", p), place, place, r.a_s.at[p], r.a_r.at[p], link.across)
        for j in range(1, minor):
            sems = r.b_s.at[p, j - 1], r.b_r.at[p, j - 1]
            go(("b", p, j), place, place, *sems, link.beside[j - 1])
        to_partner(0, link.chip, p)

    def stage_two(p):
        other = link.dest(1, 0)
        kept["a", p].wait_recv()
        if p % 2 == 0:
            for j in range(1, minor):
                place = block(other, p)
                sems = r.d_s.at[p, j - 1], r.d_r.at[p, j - 1]
                go(("d", p, j), place, place, *sems, link.beside[j - 1])
        to_partner(1, other, p)
        for j in range(1, minor):
            kept["b", p, j].wait_recv()
            if p % 2:
                place = block(link.behind(0, j), p)
                sems = r.d_s.at[p, j - 1], r.d_r.at[p, j - 1]
                go(("d", p, j), place, place, *sems, link.across)
            to_partner(1 + j, link.behind(0, j), p)

    def stage_three(p):
        for j in range(1, minor):
            kept["d", p, j].wait_recv()
            to_partner(minor + j, link.behind(1, j), p)

    order = [(k, j) for k in range(2) for j in range(minor)]

    def compute(p):
        i, c = pieces[p]
        for slot in range(half):
            kept["p", p, slot].wait_recv()
        s = link.nearest(i)
        places = [2 * link.dest(k, j) + 1 - core for k, j in order]
        places += [2 * link.dest(k, j) + core for k, j in order]

        def rows_of(ref):
            return jnp.concatenate([ref[place, s, slab(c)] for place in places], axis=0)

        turn = late.index(p)
        if turn >= 2:
            kept["o", late[turn - 2]].wait_send()

        def put(value, low):
            value = value.astype(jnp.bfloat16)
            here = pl.ds(low, value.shape[1])
            for at, (k, j) in enumerate(order):
                r.outbox[turn % 2, k, j, :, here] = value[at * chunk : (at + 1) * chunk]
                own = value[(half + at) * chunk : (half + at + 1) * chunk]
                r.paired[p, k, j, :, here] = own

        x = rows_of(tokens)
        share = softmax_rows(dot_nn(x, r.router[...]))
        share = share * rows_of(r.chosen)[:, :EXPERTS].astype(jnp.float32)
        weights = dot_split(share, r.select[...])
        gate_pre = dot_nt(x, r.gate[...])
        up_pre = dot_nt(x, r.up[...])
        sigma = jax.nn.sigmoid(gate_pre)
        silu = gate_pre * sigma
        activated = silu * up_pre
        low = 0
        if forward or backward:
            weighted = (weights * activated).astype(jnp.bfloat16)
        if backward:
            g = rows_of(grads)
            back = dot_nt(g, r.down[...])
            put(dot_split(activated * back, r.gather[...]), width)
            act_grad = weights * back
            gate_rows = act_grad * up_pre * sigma * (1.0 + gate_pre * (1.0 - sigma))
            gate_rows = gate_rows.astype(jnp.bfloat16)
            up_rows = (act_grad * silu).astype(jnp.bfloat16)
            put(dot_nn(gate_rows, r.gate[...]) + dot_nn(up_rows, r.up[...]), 0)
            low = width + 128
        if forward:
            put(dot_nn(weighted, r.down[...]), low)
        kept["o", p] = remote(
            r.outbox.at[turn % 2], r.pairs.at[p], r.o_s.at[p], r.o_r.at[p], link.partner
        )
        kept["o", p].start()
        if backward:
            pairs = (r.gate_grad, gate_rows, x), (r.up_grad, up_rows, x), (r.down_grad, weighted, g)
            for ref, left, right in pairs:
                add_up(turn, ref, dot_tn(left, right))

    def rs_one(p):
        kept["o", p].wait_recv()
        value = r.paired[p].astype(jnp.float32) + r.pairs[p].astype(jnp.float32)
        r.paired[p] = value.astype(jnp.bfloat16)
        q = p // 2
        if p % 2 == 0:
            sems = r.fa_s.at[q], r.fa_r.at[q]
            go(("f", p), r.paired.at[p, 1], r.first_a.at[q], *sems, link.across)
        else:
            for j in range(1, minor):
                sems = r.fb_s.at[q, j - 1], r.fb_r.at[q, j - 1]
                source, target = r.paired.at[p, :, j], r.first_b.at[q, j - 1]
                go(("f", p, j), source, target, *sems, link.beside[j - 1])

    def rs_two(p):
        q = p // 2
        if p % 2 == 0:
            kept["f", p].wait_recv()
            value = r.paired[p, 0].astype(jnp.float32) + r.first_a[q].astype(jnp.float32)
            r.paired[p, 0] = value.astype(jnp.bfloat16)
            for j in range(1, minor):
                sems = r.sb_s.at[q, j - 1], r.sb_r.at[q, j - 1]
                source, target = r.paired.at[p, 0, j], r.second_b.at[q, j - 1]
                go(("s", p, j), source, target, *sems, link.beside[j - 1])
        else:
            value = r.paired[p, :, 0].astype(jnp.float32)
            for j in range(1, minor):
                kept["f", p, j].wait_recv()
                value = value + r.first_b[q, j - 1].astype(jnp.float32)
            r.paired[p, :, 0] = value.astype(jnp.bfloat16)
            sems = r.sa_s.at[q], r.sa_r.at[q]
            go(("s", p), r.paired.at[p, 1, 0], r.second_a.at[q], *sems, link.across)

    def rs_three(p):
        i, c = pieces[p]
        q = p // 2
        value = r.paired[p, 0, 0].astype(jnp.float32)
        if p % 2 == 0:
            for j in range(1, minor):
                kept["s", p, j].wait_recv()
                value = value + r.second_b[q, j - 1].astype(jnp.float32)
        else:
            kept["s", p].wait_recv()
            value = value + r.second_a[q].astype(jnp.float32)
        r.total[p] = value.astype(jnp.bfloat16)
        if i:
            s = link.nearest(i)
            slot = lax.rem(s - z + t, t) - 1
            go(
                ("z", p),
                r.total.at[p],
                r.last.at[slot, c],
                r.last_s.at[slot, c],
                r.last_r.at[slot, c],
                (me, s),
            )

    arriving = []

    def rs_four(p):
        i, c = pieces[p]
        if i:
            return
        value = r.total[p].astype(jnp.float32)
        for d in range(1, t):
            remote(
                r.total.at[p],
                r.last.at[d - 1, c],
                r.last_s.at[d - 1, c],
                r.last_r.at[d - 1, c],
                link.line[d - 1],
            ).wait_recv()
            value = value + r.last[d - 1, c].astype(jnp.float32)
        for at, result in enumerate(after(c, slab(c), value, r)):
            target = r.get("shared%d" % at).at[z, slab(c)]
            target[...] = result
            arriving.extend(share_line(link, target, r.post_s.at[at, c], r.post_r.at[at, c]))

    late = list(range(chunks, len(pieces))) + list(range(chunks))
    numbers = list(range(len(pieces)))
    skip = min(chunks, len(pieces) - chunks)
    schedule = [(0, stage_one, numbers), (2, stage_two, numbers), (4, stage_three, numbers)]
    schedule += [(10 + skip, rs_three, late), (10 + skip, rs_four, late), (8 + skip, rs_two, late)]
    schedule += [(6 + skip, rs_one, late), (4 + skip, compute, late)]
    for step in range(len(pieces) + 10 + skip):
        for lag, stage, which in schedule:
            if 0 <= step - lag < len(pieces):
                stage(which[step - lag])

    for copy in arriving:
        copy.wait_recv()
    for copy in sent + arriving:
        copy.wait_send()
    for p in late[-2:]:
        kept["o", p].wait_send()


def call(kernel, operands, results, scratch, collective_id):
    vmem = pl.BlockSpec(memory_space=pltpu.VMEM)
    found = pl.pallas_call(
        functools.partial(kernel, list(operands) + list(results) + list(scratch)),
        out_shape=list(results.values()),
        in_specs=[vmem] * len(operands),
        out_specs=[vmem] * len(results),
        scratch_shapes=list(scratch.values()),
        compiler_params=pltpu.CompilerParams(
            collective_id=collective_id, has_side_effects=True, vmem_limit_bytes=56 * 2**20
        ),
    )(*operands.values())
    return dict(zip(results, found))


def both(name, *shape):
    sems = pltpu.SemaphoreType.DMA(shape)
    return {name + "_s": sems, name + "_r": sems}


def bf16(*shape):
    return jax.ShapeDtypeStruct(shape, jnp.bfloat16)


def f32(*shape):
    return jax.ShapeDtypeStruct(shape, jnp.float32)


def line_call(part, dense, operands, results, finish, chunk, collective_id):
    n, t = lax.axis_size("dp"), lax.axis_size("tensor")
    rows, width = part.shape[0] // t, part.shape[1]
    chunk = min(chunk, rows)
    chunks = rows // chunk
    scratch = dict(pre=pltpu.VMEM((t - 1, rows, width), jnp.bfloat16))
    scratch |= both("pre", t - 1, chunks) | both("post", chunks, t - 1)
    height, across = dense.shape[0] // n, dense.shape[1]
    scratch |= dict(slots=pltpu.VMEM((n - 1, height, across), jnp.bfloat16)) | both("w", n - 1)
    kernel = lambda names, *refs: line_kernel(n, t, rows, chunk, finish, names, *refs)
    operands = dict(part=part.reshape(t, rows, width)) | operands
    operands |= dict(dense=dense.reshape(n, height, across))
    results = dict(shared=bf16(t, rows, width), dense_out=f32(height, across)) | results
    return call(kernel, operands, results, scratch, collective_id)


def moe_call(
    part, operands, results, before, after, forward, backward, shared, chunk, collective_id
):
    n, t = lax.axis_size("dp"), lax.axis_size("tensor")
    rows, width = part.shape[0] // t, part.shape[1]
    chunk = min(chunk, rows)
    chunks, half, minor = rows // chunk, n // 2, n // 4
    count = t * chunks
    even, odd = (count + 1) // 2, max(count // 2, 1)
    total = (width if forward else 0) + (width + 128 if backward else 0)
    hidden = operands["gate"].shape[0]
    slots = lambda *lead: pltpu.VMEM(lead + (chunk, total), jnp.bfloat16)
    scratch = dict(
        pre=pltpu.VMEM((t - 1, rows, width), jnp.bfloat16),
        outbox=slots(2, 2, minor),
        paired=slots(count, 2, minor),
        pairs=slots(count, 2, minor),
        first_a=slots(even, minor),
        first_b=slots(odd, minor - 1, 2),
        second_a=slots(odd),
        second_b=slots(even, minor - 1),
        total=slots(count),
        last=slots(t - 1, chunks),
    )
    scratch |= both("pre", t - 1, chunks) | both("zg", chunks, t - 1) | both("p", count, half)
    scratch |= both("a", count) | both("b", count, minor - 1) | both("d", count, minor - 1)
    scratch |= both("o", count) | both("fa", even) | both("fb", odd, minor - 1)
    scratch |= both("sa", odd) | both("sb", even, minor - 1) | both("last", t - 1, chunks)
    scratch |= both("post", shared, chunks, t - 1)
    everywhere = lambda depth: bf16(n, t, rows, depth)
    found = dict(gathered=everywhere(width))
    if backward:
        found |= dict(gate_grad=f32(hidden, width), up_grad=f32(hidden, width))
        found |= dict(down_grad=f32(hidden, width))
    found |= {"shared%d" % at: bf16(t, rows, width) for at in range(shared)}
    kernel = lambda names, *refs: moe_kernel(
        n, t, rows, chunk, forward, backward, before, after, names, *refs
    )
    operands = dict(part=part.reshape(t, rows, width)) | operands
    return call(kernel, operands, found | results, scratch, collective_id)


def plane_kernel(n, names, *refs):
    r = Refs(zip(names, refs))
    me, z = lax.axis_index("dp"), lax.axis_index("tensor")
    others = [(lax.rem(me + d, n), z) for d in range(1, n)]
    barrier = pltpu.get_barrier_semaphore()
    for device in others:
        pl.semaphore_signal(barrier, inc=1, device_id=device, device_id_type=MESH)
    pl.semaphore_wait(barrier, n - 1)
    copies = [
        remote(r.block, r.everything.at[me], r.b_s.at[d], r.b_r.at[d], device)
        for d, device in enumerate(others)
    ]
    for copy in copies:
        copy.start()
    r.everything[me] = r.block[...]
    for copy in copies:
        copy.wait()


def plane_call(block, collective_id):
    n = lax.axis_size("dp")
    kernel = lambda names, *refs: plane_kernel(n, names, *refs)
    results = dict(everything=bf16(n, *block.shape))
    return call(kernel, dict(block=block), results, both("b", n - 1), collective_id)["everything"]


def spread_kernel(n, t, names, *refs):
    r = Refs(zip(names, refs))
    link = Link(n, t)
    me = link.me
    others = [(lax.rem(me + d, n), link.z) for d in range(1, n)]
    barrier = pltpu.get_barrier_semaphore()
    for device in link.line + others:
        pl.semaphore_signal(barrier, inc=1, device_id=device, device_id_type=MESH)
    pl.semaphore_wait(barrier, len(link.line) + len(others))
    copies = []
    for d, device in enumerate(link.line):
        copies.append(remote(r.gain, r.gains.at[d], r.g_s.at[d], r.g_r.at[d], device))
        copies.append(remote(r.side, r.sides.at[d], r.d_s.at[d], r.d_r.at[d], device))
    for copy in copies:
        copy.start()
    value = r.gain[...]
    for d in range(t - 1):
        copies[2 * d].wait_recv()
        value = value + r.gains[d]
    r.summed[...] = value
    outward = []
    for d, device in enumerate(others):
        source = r.summed.at[device[0]]
        outward.append(remote(source, r.slices.at[d], r.o_s.at[d], r.o_r.at[d], device))
        outward[-1].start()
    value = r.side[...]
    for d in range(t - 1):
        copies[2 * d + 1].wait_recv()
        value = value + r.sides[d]
    r.side_out[...] = value
    value = r.summed[me]
    for d in range(n - 1):
        outward[d].wait_recv()
        value = value + r.slices[d]
    r.gain_out[...] = value
    for copy in copies + outward:
        copy.wait_send()


def spread_call(side, gain, collective_id):
    n, t = lax.axis_size("dp"), lax.axis_size("tensor")
    layers, width = gain.shape[0], gain.shape[1] // n
    gain = gain.reshape(layers, n, width).transpose(1, 0, 2)
    gain = jnp.pad(gain, ((0, 0), (0, 8 - layers), (0, 0)))
    vmem = lambda *shape: pltpu.VMEM(shape, jnp.float32)
    scratch = dict(
        gains=vmem(t - 1, n, 8, width),
        sides=vmem(t - 1, *side.shape),
        summed=vmem(n, 8, width),
        slices=vmem(n - 1, 8, width),
    )
    scratch |= both("g", t - 1) | both("d", t - 1) | both("o", n - 1)
    results = dict(side_out=f32(*side.shape), gain_out=f32(8, width))
    kernel = lambda names, *refs: spread_kernel(n, t, names, *refs)
    found = call(kernel, dict(side=side, gain=gain), results, scratch, collective_id)
    return found["side_out"], found["gain_out"][:layers]


def row_norm(source, gain):
    scale = lax.rsqrt(jnp.mean(source * source, axis=1, keepdims=True) + EPSILON)
    return scale, source * scale * gain


def row_norm_backward(grad_in, source, gain):
    scale = lax.rsqrt(jnp.mean(source * source, axis=1, keepdims=True) + EPSILON)
    gain_grad = jnp.sum(grad_in * source * scale, axis=0, keepdims=True)
    scaled = grad_in * gain
    inner = jnp.mean(scaled * source, axis=1, keepdims=True)
    return scale * (scaled - source * scale * scale * inner), gain_grad


def add_up(c, ref, value):
    ref[...] = value if c == 0 else ref[...] + value


def attention_done(c, here, value, r):
    middle = r.inputs[here] + RESIDUAL_SCALE * value
    r.middle[here] = middle
    return row_norm(middle, r.mixture_gain[...])[1].astype(jnp.bfloat16)


def layer_done(c, here, value, r):
    output = r.middle[here] + RESIDUAL_SCALE * value
    r.output[here] = output
    return (row_norm(output, r.next_gain[...])[1].astype(jnp.bfloat16),)


def mixture_backward_done(c, here, value, r):
    width, count = r.middle.shape[1], r.router.shape[1]
    link_me, z = lax.axis_index("dp"), lax.axis_index("tensor")
    tokens = r.tokens if hasattr(r, "tokens") else r.gathered
    share = softmax_rows(dot_nn(tokens[link_me, z, here], r.router[...]))
    prob_grad = r.chosen[link_me, z, here][:, :EXPERTS].astype(jnp.float32) * value[:, width : width + count]
    logit_grad = share * (prob_grad - jnp.sum(share * prob_grad, axis=1, keepdims=True))
    second_grad = value[:, :width] + dot_full(logit_grad, r.router_t[...])
    middle = r.middle[here]
    norm_grad, gain_grad = row_norm_backward(second_grad, middle, r.mixture_gain[...])
    grad_out = r.grad if hasattr(r, "grad") else r.grad_out
    middle_grad = grad_out[here] + norm_grad
    r.middle_grad[here] = middle_grad
    r.logit_grad[here] = logit_grad
    add_up(c, r.mixture_gain_grad, gain_grad)
    results = ((RESIDUAL_SCALE * middle_grad).astype(jnp.bfloat16),)
    if value.shape[1] > width + 128:
        last = middle + RESIDUAL_SCALE * value[:, width + 128 :]
        results += (last.astype(jnp.bfloat16),)
    return results


def attention_backward_done(scale, c, here, value, r):
    norm_grad, gain_grad = row_norm_backward(value, r.inputs[here], r.attention_gain[...])
    grad = r.upper_grad[here] + norm_grad
    r.grad[here] = grad
    add_up(c, r.attention_gain_grad, gain_grad)
    return (scale * grad).astype(jnp.bfloat16)


def own_rows(array, offset=0):
    rows = SEQ // lax.axis_size("tensor")
    return lax.dynamic_slice_in_dim(array, offset + lax.axis_index("tensor") * rows, rows, axis=0)


def attention_forward(first_input, params, cosine, sine):
    query_weight, key_weight, value_weight, output_weight = params[1:5]
    row_count = first_input.shape[0]
    query_heads = query_weight.shape[1] // HD
    key_heads = key_weight.shape[0] // HD
    group_size = query_heads // key_heads
    seq_count = row_count // SEQ
    query = jnp.dot(first_input, query_weight, preferred_element_type=jnp.float32).reshape(
        row_count, query_heads, HD
    )
    keys = jnp.dot(first_input, key_weight.T, preferred_element_type=jnp.float32).reshape(
        row_count, key_heads, HD
    )
    values = jnp.dot(first_input, value_weight.T, preferred_element_type=jnp.float32).astype(
        jnp.bfloat16
    )
    query = (query * cosine + rotate_half(query) * sine).astype(jnp.bfloat16)
    keys = (keys * cosine + rotate_half(keys) * sine).astype(jnp.bfloat16)
    query_split = query.reshape(seq_count, SEQ, key_heads, group_size, HD)
    key_split = keys.reshape(seq_count, SEQ, key_heads, HD)
    value_split = values.reshape(seq_count, SEQ, key_heads, HD)
    attended, log_total = attend_forward(query_split, key_split, value_split)
    attended_rows = attended.reshape(row_count, query_heads * HD)
    part = jnp.dot(attended_rows, output_weight, preferred_element_type=jnp.float32)
    return part.astype(jnp.bfloat16), (query_split, key_split, value_split, attended, log_total)


def attention_backward(attention_grad, first_input, saved, params, cosine, sine):
    query_weight, key_weight, value_weight, output_weight = params[1:5]
    query_split, key_split, value_split, attended, log_total = saved
    row_count, width = attention_grad.shape
    query_heads = query_weight.shape[1] // HD
    key_heads = key_weight.shape[0] // HD
    attended_rows = attended.reshape(row_count, query_heads * HD)
    output_grad = jnp.dot(attention_grad.T, attended_rows, preferred_element_type=jnp.float32)
    attended_grad = jnp.dot(
        attention_grad, output_weight.T, preferred_element_type=jnp.float32
    ).astype(jnp.bfloat16)
    query_grad, key_grad, value_grad = attend_backward(
        query_split,
        key_split,
        value_split,
        attended,
        log_total,
        attended_grad.reshape(attended.shape),
    )
    query_grad = query_grad.reshape(row_count, query_heads, HD)
    query_grad = (
        (query_grad * cosine - rotate_half(query_grad) * sine)
        .astype(jnp.bfloat16)
        .reshape(row_count, query_heads * HD)
    )
    key_grad = key_grad.reshape(row_count, key_heads, HD)
    key_grad = (
        (key_grad * cosine - rotate_half(key_grad) * sine)
        .astype(jnp.bfloat16)
        .reshape(row_count, key_heads * HD)
    )
    value_grad = value_grad.astype(jnp.bfloat16).reshape(row_count, key_heads * HD)
    first_part = (
        jnp.dot(query_grad, query_weight.T, preferred_element_type=jnp.float32)
        + jnp.dot(key_grad, key_weight, preferred_element_type=jnp.float32)
        + jnp.dot(value_grad, value_weight, preferred_element_type=jnp.float32)
    ).astype(jnp.bfloat16)
    projected = jnp.dot(
        first_input.T,
        jnp.concatenate([query_grad, key_grad, value_grad], axis=1),
        preferred_element_type=jnp.float32,
    )
    return first_part, jnp.concatenate([projected, output_grad], axis=1)


def shards(
    hidden_states,
    output_cotangent,
    routes,
    attention_gain,
    query_weight,
    key_weight,
    value_weight,
    output_weight,
    mixture_gain,
    router_weight,
    gate_weight,
    up_weight,
    down_weight,
):
    params_all = (
        attention_gain,
        query_weight,
        key_weight,
        value_weight,
        output_weight,
        mixture_gain,
        router_weight,
        gate_weight,
        up_weight,
        down_weight,
    )
    n, t = lax.axis_size("dp"), lax.axis_size("tensor")
    row_count, width = hidden_states.shape
    rows = row_count // t
    layer_count = query_weight.shape[0]
    cosine, sine = rope_tables(row_count)
    local_experts, hidden = gate_weight.shape[1:3]
    expert_ids = jnp.arange(EXPERTS, dtype=jnp.int32)
    chosen = jnp.any(routes[:, :, None] == expert_ids[None, None, :], axis=1)
    first = (RESIDUAL_SCALE * output_cotangent).astype(jnp.bfloat16)
    side = jnp.pad(chosen.astype(jnp.bfloat16), ((0, 0), (0, 128 - EXPERTS)))
    chosen_all = plane_call(side, 32)
    first, chosen_all = lax.optimization_barrier((first, chosen_all))
    cotangents = lax.all_gather(first, "dp", axis=0, tiled=True)
    everywhere = lambda array: array.reshape(n, t, rows, array.shape[-1])
    owners = lax.axis_index("dp") * local_experts + jnp.arange(local_experts * hidden) // hidden
    select = (expert_ids[:, None] == owners[None, :]).astype(jnp.bfloat16)
    gather = jnp.pad(select.T, ((0, 0), (0, 128 - EXPERTS)))
    params = [tuple(weight[i] for weight in params_all) for i in range(layer_count)]
    gains = lambda i, kind: params[i][kind][None, :]
    chosen_all = everywhere(chosen_all)

    def shared_operands(i):
        flat = lambda array: array.reshape(local_experts * hidden, width)
        return dict(
            router=params[i][6],
            gate=flat(params[i][7]),
            up=flat(params[i][8]),
            down=flat(params[i][9]),
            select=select,
            gather=gather,
            chosen=chosen_all,
        )

    first_input = row_norm(hidden_states, gains(0, 0))[1].astype(jnp.bfloat16)
    current = own_rows(hidden_states)
    kept = []
    backward_operands = lambda i: dict(
        router_t=params[i][6].astype(jnp.float32).T,
        mixture_gain=gains(i, 5),
    )
    backward_results = dict(
        middle_grad=f32(rows, width),
        logit_grad=f32(rows, EXPERTS),
        mixture_gain_grad=f32(1, width),
    )
    for i in range(layer_count):
        part, heads = attention_forward(first_input, params[i], cosine, sine)
        operands = shared_operands(i) | dict(inputs=current, mixture_gain=gains(i, 5))
        results = dict(middle=f32(rows, width))
        if i + 1 < layer_count:
            found = moe_call(
                part,
                operands | dict(next_gain=gains(i + 1, 0)),
                results | dict(output=f32(rows, width)),
                attention_done,
                layer_done,
                True,
                False,
                1,
                32,
                1 + i,
            )
            kept.append((first_input, current, heads, found))
            first_input = found["shared0"].reshape(row_count, width)
            current = found["output"]
        else:
            found = moe_call(
                part,
                operands
                | backward_operands(i)
                | dict(
                    grads=everywhere(cotangents),
                    grad_out=own_rows(output_cotangent),
                ),
                results | backward_results,
                attention_done,
                mixture_backward_done,
                True,
                True,
                2,
                32,
                1 + i,
            )
            kept.append((first_input, current, heads, found))
            last = found["shared1"].reshape(row_count, width)
    dense_layers = [None] * layer_count
    expert_layers = [None] * layer_count
    grads = everywhere(cotangents)
    for i in reversed(range(layer_count)):
        first_input, current, heads, ahead = kept[i]
        tokens = ahead["gathered"]
        if i + 1 < layer_count:
            found = moe_call(
                part,
                shared_operands(i)
                | backward_operands(i)
                | dict(
                    tokens=tokens,
                    middle=ahead["middle"],
                    inputs=upper_inputs,
                    attention_gain=gains(i + 1, 0),
                    upper_grad=found["middle_grad"],
                ),
                backward_results | dict(grad=f32(rows, width), attention_gain_grad=f32(1, width)),
                functools.partial(attention_backward_done, RESIDUAL_SCALE),
                mixture_backward_done,
                False,
                True,
                1,
                32,
                11 + i,
            )
            grads = found["gathered"]
            gain_grads = [found["attention_gain_grad"]] + gain_grads
        else:
            found = ahead
            gain_grads = []
        part, dense_layers[i] = attention_backward(
            found["shared0"].reshape(row_count, width), first_input, heads, params[i], cosine, sine
        )
        upper_inputs = current
        flat = lambda array: array.reshape(n * row_count, array.shape[-1])
        shape = gate_weight.shape[1:]
        expert_layers[i] = [
            found[name].reshape(shape) for name in ("gate_grad", "up_grad", "down_grad")
        ]
        own_second = own_rows(flat(tokens), lax.axis_index("dp") * SEQ).astype(jnp.float32)
        small = jnp.concatenate(
            [
                dot_full(own_second.T, found["logit_grad"]),
                found["mixture_gain_grad"].T,
                jnp.zeros((width, 127 - EXPERTS), jnp.float32),
            ],
            axis=1,
        )
        dense = jnp.concatenate([dense_layers[i], small], axis=1).astype(jnp.bfloat16)
        if i:
            part, dense = lax.optimization_barrier((part, dense))
            dense = lax.psum_scatter(dense, "dp", scatter_dimension=0, tiled=True)
            dense_layers[i] = dense.astype(jnp.float32)
    tail = line_call(
        part,
        dense,
        dict(
            inputs=upper_inputs,
            attention_gain=gains(0, 0),
            upper_grad=found["middle_grad"],
        ),
        dict(grad=f32(rows, width), attention_gain_grad=f32(1, width)),
        functools.partial(attention_backward_done, 1.0),
        32,
        21,
    )
    gain_grads = [tail["attention_gain_grad"]] + gain_grads
    dense_layers[0] = tail["dense_out"]
    sides = [dense[:, -128 : 40 - 128].T for dense in dense_layers]
    q, k = query_weight.shape[2], key_weight.shape[1]
    dense_layers = [
        (
            dense[:, :q],
            dense[:, q : q + k].T,
            dense[:, q + k : q + 2 * k].T,
            dense[:, q + 2 * k : 2 * q + 2 * k].T,
        )
        for dense in dense_layers
    ]
    sides, attention_gains = spread_call(
        jnp.concatenate(sides, axis=0), jnp.concatenate(gain_grads, axis=0), 31
    )
    sides = sides.reshape(layer_count, 40, -1)
    dense = [jnp.stack([entry[position] for entry in dense_layers]) for position in range(4)]
    stacked = [attention_gains, *dense, sides[:, EXPERTS], sides[:, :EXPERTS].transpose(0, 2, 1)]
    stacked += [jnp.stack([entry[position] for entry in expert_layers]) for position in range(3)]
    result = tail["shared"].reshape(row_count, width)
    return (last.astype(jnp.float32), result.astype(jnp.float32), *stacked)


def solution(mesh):
    placed = (
        P("dp", None),
        P("dp", None),
        P("dp", None),
        P(),
        P(None, None, "tensor"),
        P(None, "tensor", None),
        P(None, "tensor", None),
        P(None, "tensor", None),
        P(),
        P(),
        P(None, "dp", "tensor", None),
        P(None, "dp", "tensor", None),
        P(None, "dp", "tensor", None),
    )
    return jax.shard_map(
        shards,
        mesh=mesh,
        in_specs=placed,
        out_specs=(
            P("dp", None),
            P("dp", None),
            P(None, "dp"),
            P(None, "dp", "tensor"),
            P(None, "tensor", "dp"),
            P(None, "tensor", "dp"),
            P(None, "tensor", "dp"),
            P(None, "dp"),
            P(None, "dp", None),
            P(None, "dp", "tensor", None),
            P(None, "dp", "tensor", None),
            P(None, "dp", "tensor", None),
        ),
        check_vma=False,
    )
```
